32 devices in a mesh: ty: 4 (over y, x), tx: 4 (over z), corner: 2 (over core).
Axes of the slice: x: 2, y: 2, z: 4, core: 2. Of those that a mesh axis runs over, the one named last changes fastest.
Arguments:
- level_init: int32 [1024, 1024], P('ty', 'tx'), may hold values from -64 to 64
- target: int32 [1024, 1024], P('ty', 'tx'), may hold values 0 or 1
- kernels: float32 [2, 5, 2, 128, 128], P('corner'), may hold values from -12 to 12
- corner_doses: float32 [2], P('corner'), may hold values from 0.7 to 1.4
Outputs:
- resist: float32 [2, 1024, 1024], P('corner', 'ty', 'tx')
- level_set: float32 [1024, 1024], P('ty', 'tx')
The draws below stay inside these ranges and needn't reach their ends.
All inputs are finite; a program needn't handle non-finite values. No bound on the sum of `target` on one device may be relied on, other than what follows from the above.
Results may differ from the reference program's by a relative error of at most 0.015.
The reference program's roundings to bfloat16 on the way count: a program that leaves them out, or rounds other values in their place, can miss the bound.
Values may be sent and summed in bfloat16 or wider, within the bound.
No kernel may reach another device: no remote copies, remote signals or barrier semaphores. Data moves between devices by JAX's collectives and lax.ppermute only.
A program may use at most 64 MiB of HBM per device.

```python
import math
import jax
import jax.numpy as jnp
from jax import lax

TILE = 256
HALO = 128
KF = 128
KERNELS = 5
LS_STEPS = 3
WIN = 512
NY = 1024
NX = 1024
CORNERS = 2
N_TY = 4
N_TX = 4


def place_ends(values, rng, smallest, high):
    shape = values.shape
    spot = [jax.random.randint(jax.random.fold_in(rng, axis), (), 0, shape[axis]) for axis in range(len(shape))]
    values = values.at[tuple(spot)].set(smallest)
    longest = shape.index(max(shape))
    spot[longest] = (spot[longest] + 1) % shape[longest]
    return values.at[tuple(spot)].set(high)


def level_of(stream_key, dims, shards, low, top_value):
    level = 1.0
    for axis_at, shards_of in shards:
        steps = jax.random.uniform(jax.random.fold_in(jax.random.fold_in(stream_key, 6), axis_at), (shards_of,), jnp.float32, low / len(shards), top_value / len(shards))
        level = level * jnp.repeat(jnp.exp(steps), dims[axis_at] // shards_of).reshape((-1,) + (1,) * (len(dims) - 1 - axis_at))
    return level


def gaussian(rng, shape, scale, most, pieces=(), held_as=jnp.bfloat16):
    entries = scale * jax.random.normal(rng, shape, jnp.float32)
    if pieces:
        entries = entries * level_of(rng, shape, pieces, -0.22, 0.18)
    return jnp.clip(entries, -most, most).astype(held_as)


def setup_inputs(seed: int = 0) -> dict:
    streams_of = jax.random.split(jax.random.key(seed), 5)
    level_init = place_ends(jax.random.randint(streams_of[0], (NY, NX), -64, 65), jax.random.fold_in(streams_of[0], 1), -64, 64).astype(jnp.int32)
    target = place_ends((jax.random.randint(streams_of[1], (NY, NX), 0, 2) < 1).astype(jnp.int32), jax.random.fold_in(streams_of[1], 1), 0, 1)
    kernels = gaussian(streams_of[2], (CORNERS, KERNELS, 2, KF, KF), 2.0, 12.0, ((0, 2),), jnp.float32)
    corner_doses = jnp.clip(jnp.exp(math.log(1.4) - 0.6931472 * jax.random.uniform(streams_of[3], (CORNERS,), jnp.float32) ** level_of(streams_of[3], (CORNERS,), ((0, 2),), -0.2, 0.2)), 0.7, 1.4)
    return dict(level_init=level_init, target=target, kernels=kernels, corner_doses=corner_doses)


STEEPNESS = 4.0
THRESHOLD = 1.0
SPEED_GAIN = 4.0
SMOOTHING = 0.24
GRAD_FLOOR = 0.25

def make_tables(window, freqs, margin, tile):
    shifts = jnp.arange(freqs, dtype=jnp.int32) - freqs // 2
    places = jnp.arange(window, dtype=jnp.int32)
    phases = shifts[:, None] * places[None, :] % window
    angles = 2.0 * math.pi / window * phases.astype(jnp.float32)
    scaled = 1.0 / math.sqrt(window)
    fwd_cos = (jnp.cos(angles) * scaled).astype(jnp.bfloat16)
    fwd_sin = (-jnp.sin(angles) * scaled).astype(jnp.bfloat16)
    inner = angles[:, margin:margin + tile].T
    inv_cos = (jnp.cos(inner) * scaled).astype(jnp.bfloat16)
    inv_sin = (jnp.sin(inner) * scaled).astype(jnp.bfloat16)
    return (fwd_cos, fwd_sin, inv_cos, inv_sin)

def matmul(left, right):
    return jnp.dot(left, right, preferred_element_type=jnp.float32)

def batched(form, left, right):
    return jnp.einsum(form, left.astype(jnp.float32), right.astype(jnp.float32), precision=lax.Precision.HIGHEST)

def tile_pass(win_data, goal, kernel_re, kernel_im, doses_col, tables):
    fwd_cos, fwd_sin, inv_cos, inv_sin = tables
    freqs = fwd_cos.shape[0]
    lift = matmul(jnp.concatenate([fwd_cos, fwd_sin], axis=0), win_data).astype(jnp.bfloat16)
    lift_re = lift[:freqs]
    lift_im = lift[freqs:]
    spec_re = matmul(lift_re, fwd_cos.T) - matmul(lift_im, fwd_sin.T)
    spec_im = matmul(lift_re, fwd_sin.T) + matmul(lift_im, fwd_cos.T)
    blur_re = (kernel_re * spec_re - kernel_im * spec_im).astype(jnp.bfloat16)
    blur_im = (kernel_re * spec_im + kernel_im * spec_re).astype(jnp.bfloat16)
    proj_re = (batched('rj,gjk->grk', inv_cos, blur_re) - batched('rj,gjk->grk', inv_sin, blur_im)).astype(jnp.bfloat16)
    proj_im = (batched('rj,gjk->grk', inv_cos, blur_im) + batched('rj,gjk->grk', inv_sin, blur_re)).astype(jnp.bfloat16)
    field_re = batched('grj,cj->grc', proj_re, inv_cos) - batched('grj,cj->grc', proj_im, inv_sin)
    field_im = batched('grj,cj->grc', proj_re, inv_sin) + batched('grj,cj->grc', proj_im, inv_cos)
    groups = doses_col.shape[0]
    tile = field_re.shape[1]
    grouped = (groups, -1, tile, tile)
    power = (field_re * field_re + field_im * field_im).reshape(grouped)
    intensity = lax.optimization_barrier(jnp.sum(power, axis=1))
    dose_col = doses_col[:, None, None]
    resist = jax.nn.sigmoid(STEEPNESS * (dose_col * intensity - THRESHOLD))
    sens = 2.0 * (resist - goal) * STEEPNESS * dose_col * resist * (1.0 - resist)
    adj_re = (2.0 * sens[:, None] * field_re.reshape(grouped)).reshape(field_re.shape).astype(jnp.bfloat16)
    adj_im = (2.0 * sens[:, None] * field_im.reshape(grouped)).reshape(field_im.shape).astype(jnp.bfloat16)
    back_re = (batched('grc,cj->grj', adj_re, inv_cos) + batched('grc,cj->grj', adj_im, inv_sin)).astype(jnp.bfloat16)
    back_im = (batched('grc,cj->grj', adj_im, inv_cos) - batched('grc,cj->grj', adj_re, inv_sin)).astype(jnp.bfloat16)
    grad_blur_re = batched('rj,grk->gjk', inv_cos, back_re) + batched('rj,grk->gjk', inv_sin, back_im)
    grad_blur_im = batched('rj,grk->gjk', inv_cos, back_im) - batched('rj,grk->gjk', inv_sin, back_re)
    grad_spec_re = lax.optimization_barrier(jnp.sum(kernel_re * grad_blur_re + kernel_im * grad_blur_im, axis=0))
    grad_spec_im = lax.optimization_barrier(jnp.sum(kernel_re * grad_blur_im - kernel_im * grad_blur_re, axis=0))
    return (resist, grad_spec_re, grad_spec_im)

def window_grad(grad_spec_re, grad_spec_im, tables):
    fwd_cos, fwd_sin = (tables[0], tables[1])
    spec_low_re = grad_spec_re.astype(jnp.bfloat16)
    spec_low_im = grad_spec_im.astype(jnp.bfloat16)
    grad_lift_re = (matmul(spec_low_re, fwd_cos) + matmul(spec_low_im, fwd_sin)).astype(jnp.bfloat16)
    grad_lift_im = (matmul(spec_low_im, fwd_cos) - matmul(spec_low_re, fwd_sin)).astype(jnp.bfloat16)
    stacked = jnp.concatenate([fwd_cos, fwd_sin], axis=0)
    grad_lift = jnp.concatenate([grad_lift_re, grad_lift_im], axis=0)
    result = lax.dot_general(stacked, grad_lift, (((0,), (0,)), ((), ())), preferred_element_type=jnp.float32)
    return result.astype(jnp.bfloat16)

def advance(padded, speed):
    centre = padded[1:-1, 1:-1]
    above_cells = padded[:-2, 1:-1]
    below_cells = padded[2:, 1:-1]
    left_cells = padded[1:-1, :-2]
    right_cells = padded[1:-1, 2:]
    slope_y = 0.5 * (below_cells - above_cells)
    slope_x = 0.5 * (right_cells - left_cells)
    spread = above_cells + below_cells + left_cells + right_cells - 4.0 * centre
    return centre - SPEED_GAIN * speed * jnp.sqrt(GRAD_FLOOR + slope_y * slope_y + slope_x * slope_x) + SMOOTHING * spread

def reference(level_init, target, kernels, corner_doses):
    tile = TILE
    margin = HALO
    window = WIN
    freqs = KF
    tables = make_tables(window, freqs, margin, tile)
    level = level_init.astype(jnp.float32) * 0.125
    trans = jnp.tanh(0.25 * level)
    padded = jnp.pad(trans.astype(jnp.bfloat16), margin)
    kernel_re = kernels[:, :, 0].reshape(-1, freqs, freqs)
    kernel_im = kernels[:, :, 1].reshape(-1, freqs, freqs)
    goals = target.astype(jnp.float32)

    def per_tile(index):
        row_start = (index // N_TX * tile).astype(jnp.int32)
        col_start = (index % N_TX * tile).astype(jnp.int32)
        win_data = lax.dynamic_slice(padded, (row_start, col_start), (window, window))
        goal = lax.dynamic_slice(goals, (row_start, col_start), (tile, tile))
        resist_tile, grad_spec_re, grad_spec_im = tile_pass(win_data, goal, kernel_re, kernel_im, corner_doses, tables)
        return (resist_tile, window_grad(grad_spec_re, grad_spec_im, tables))
    count = N_TY * N_TX
    resist_all, windows = lax.map(per_tile, jnp.arange(count, dtype=jnp.int32))
    total = jnp.zeros((NY + 2 * margin, NX + 2 * margin), jnp.float32)

    def add_window(index, total):
        row_start = (index // N_TX * tile).astype(jnp.int32)
        col_start = (index % N_TX * tile).astype(jnp.int32)
        piece = windows[index].astype(jnp.float32)
        current = lax.dynamic_slice(total, (row_start, col_start), (window, window))
        return lax.dynamic_update_slice(total, current + piece, (row_start, col_start))
    total = lax.fori_loop(0, count, add_window, total)
    grad_trans = total[margin:margin + NY, margin:margin + NX]
    speed = grad_trans * 0.25 * (1.0 - trans * trans)
    for repeat in range(LS_STEPS):
        level = advance(jnp.pad(level, 1), speed)
    resist = resist_all.reshape(N_TY, N_TX, CORNERS, tile, tile).transpose(2, 0, 3, 1, 4).reshape(CORNERS, NY, NX)
    return (resist, level)
```

```python
import functools
import math

import jax
import jax.numpy as jnp
import numpy as np
from jax import lax
from jax.experimental import pallas as pl
from jax.experimental.pallas import tpu as pltpu
from jax.sharding import PartitionSpec as P

HALO = 128
KF = 128
LS_STEPS = 3

STEEPNESS = 4.0
THRESHOLD = 1.0
SPEED_GAIN = 4.0
SMOOTHING = 0.24
GRAD_FLOOR = 0.25

RIM = 16


def make_tables(tile, margin, freqs):
    window = tile + 2 * margin
    shifts = np.arange(freqs) - freqs // 2
    places = np.arange(window)
    angles = 2.0 * math.pi / window * (shifts[:, None] * places[None, :] % window)
    scaled = 1.0 / math.sqrt(window)
    cos = np.cos(angles) * scaled
    sin = np.sin(angles) * scaled
    stacked = np.concatenate([cos, -sin], axis=0)
    inv_cos = cos[:, margin : margin + tile].T
    inv_sin = sin[:, margin : margin + tile].T
    inverse = np.block([[inv_cos, -inv_sin], [inv_sin, inv_cos]])

    def rim(width, offset):
        out = np.zeros((2 * freqs, width))
        for step in range(LS_STEPS):
            for place, at in ((tile + step, step), (step - LS_STEPS, width - LS_STEPS + step)):
                if 0 <= place + offset < window:
                    out[:, at] = stacked[:, place + offset]
        return out

    offsets = (margin + tile, margin, margin - tile)
    rim_cols = np.stack([rim(margin, offset) for offset in offsets])
    rim_rows = [rim(RIM, offset).T for offset in offsets]
    own_rows = np.concatenate([stacked[:, margin : margin + tile].T, rim_rows[1]])
    send_rows = np.stack(
        [
            np.concatenate([stacked[:, tile + margin :].T, rim_rows[0]]),
            np.concatenate([stacked[:, :margin].T, rim_rows[2]]),
        ]
    )
    as_const = lambda values: np.asarray(values, np.float32).astype(jnp.bfloat16)
    return {
        "fwd": as_const(stacked),
        "fwd_t": as_const(stacked.T),
        "inv": as_const(inverse),
        "inv_t": as_const(inverse.T),
        "rim_cols": as_const(rim_cols),
        "own_rows": as_const(own_rows),
        "send_rows": as_const(send_rows),
    }


def dot(left, right):
    return jnp.dot(left, right, preferred_element_type=jnp.float32)


def dot_general(left, right, left_dim, right_dim):
    return lax.dot_general(
        left, right, (((left_dim,), (right_dim,)), ((), ())), preferred_element_type=jnp.float32
    )


def by_core(core, first, second):
    return jnp.where(core == 0, first, second)


def lift_kernel(level_ref, mine_ref, other_ref, fwd_ref, lift_ref, send_ref):
    core = lax.axis_index("corner")
    tile = level_ref.shape[0]
    margin = mine_ref.shape[0]
    level = level_ref[...].astype(jnp.float32) * 0.125
    mine = mine_ref[...].astype(jnp.float32)
    other = other_ref[...].astype(jnp.float32)
    above = by_core(core, mine, other)
    below = by_core(core, other, mine)
    squash = lambda values: jnp.tanh(0.25 * values).astype(jnp.bfloat16)
    lift = (
        dot(fwd_ref[:, :margin], squash(above))
        + dot(fwd_ref[:, margin : margin + tile], squash(level))
        + dot(fwd_ref[:, margin + tile :], squash(below))
    ).astype(jnp.bfloat16)
    lift_ref[...] = lift
    rows = lift.shape[0]
    send_ref[:rows, :] = by_core(core, lift[:, tile - margin :], lift[:, :margin])
    at = lax.broadcasted_iota(jnp.int32, (RIM, margin), 0)
    lane = lax.broadcasted_iota(jnp.int32, (RIM, margin), 1)
    first = by_core(core, margin - LS_STEPS, 0)
    pick = ((lane == first + at) & (at < LS_STEPS)).astype(jnp.bfloat16)
    rim = jnp.where(
        lax.broadcasted_iota(jnp.int32, (RIM, tile), 0) < RIM // 2,
        below[:RIM],
        above[margin - RIM :],
    )
    strip = by_core(core, level[:, tile - margin :], level[:, :margin]).astype(jnp.bfloat16)
    rim_strip = by_core(core, rim[:, tile - margin :], rim[:, :margin]).astype(jnp.bfloat16)
    for block in range(tile // margin):
        picked = dot_general(pick, strip[block * margin : (block + 1) * margin], 1, 1)
        send_ref[rows + block * RIM : rows + (block + 1) * RIM, :] = picked.astype(jnp.bfloat16)
    padded = jnp.concatenate([rim_strip, jnp.zeros((margin - RIM, margin), jnp.bfloat16)], axis=0)
    block = tile // margin
    send_ref[rows + block * RIM : rows + (block + 1) * RIM, :] = dot_general(
        pick, padded, 1, 1
    ).astype(jnp.bfloat16)


def corner_kernel(
    dose_ref,
    lift_ref,
    mine_ref,
    other_ref,
    kernels_ref,
    target_ref,
    fwd_t_ref,
    inv_ref,
    inv_t_ref,
    resist_ref,
    grad_ref,
    blur_ref,
    proj_ref,
    field_ref,
    back_ref,
):
    core = lax.axis_index("corner")
    tile = target_ref.shape[0]
    rows = lift_ref.shape[0]
    freqs = rows // 2
    margin = mine_ref.shape[1]
    count = kernels_ref.shape[0]
    mine = mine_ref[:rows, :]
    other = other_ref[:rows, :]
    mixed = (
        dot(by_core(core, mine, other), fwd_t_ref[:margin, :])
        + dot(lift_ref[...], fwd_t_ref[margin : margin + tile, :])
        + dot(by_core(core, other, mine), fwd_t_ref[margin + tile :, :])
    )
    spec_re = mixed[:freqs, :freqs] - mixed[freqs:, freqs:]
    spec_im = mixed[:freqs, freqs:] + mixed[freqs:, :freqs]
    for g in range(count):
        kernel_re = kernels_ref[g, 0]
        kernel_im = kernels_ref[g, 1]
        cols = slice(g * freqs, (g + 1) * freqs)
        blur_ref[:freqs, cols] = (kernel_re * spec_re - kernel_im * spec_im).astype(jnp.bfloat16)
        blur_ref[freqs:, cols] = (kernel_re * spec_im + kernel_im * spec_re).astype(jnp.bfloat16)
    proj_ref[...] = dot(inv_ref[...], blur_ref[...]).astype(jnp.bfloat16)
    power = jnp.zeros((tile, tile), jnp.float32)
    for g in range(count):
        cols = slice(g * freqs, (g + 1) * freqs)
        pair = jnp.concatenate([proj_ref[:tile, cols], proj_ref[tile:, cols]], axis=1)
        field = dot(pair, inv_t_ref[...])
        field_ref[g] = field
        power = power + (field[:, :tile] * field[:, :tile] + field[:, tile:] * field[:, tile:])
    dose = dose_ref[0]
    resist = jax.nn.sigmoid(STEEPNESS * (dose * power - THRESHOLD))
    resist_ref[...] = resist
    goal = target_ref[...].astype(jnp.float32)
    sens = 2.0 * (resist - goal) * STEEPNESS * dose * resist * (1.0 - resist)
    twice = 2.0 * sens
    twice = jnp.concatenate([twice, twice], axis=1)
    for g in range(count):
        cols = slice(g * freqs, (g + 1) * freqs)
        back = dot((twice * field_ref[g]).astype(jnp.bfloat16), inv_ref[...]).astype(jnp.bfloat16)
        back_ref[:tile, cols] = back[:, :freqs]
        back_ref[tile:, cols] = back[:, freqs:]
    blurred = dot(inv_t_ref[...], back_ref[...])
    grad_re = jnp.zeros((freqs, freqs), jnp.float32)
    grad_im = jnp.zeros((freqs, freqs), jnp.float32)
    for g in range(count):
        kernel_re = kernels_ref[g, 0]
        kernel_im = kernels_ref[g, 1]
        cols = slice(g * freqs, (g + 1) * freqs)
        blur_re = blurred[:freqs, cols]
        blur_im = blurred[freqs:, cols]
        grad_re = grad_re + (kernel_re * blur_re + kernel_im * blur_im)
        grad_im = grad_im + (kernel_re * blur_im - kernel_im * blur_re)
    grad_ref[:freqs, :] = grad_re
    grad_ref[freqs:, :] = grad_im


def lift_grad_kernel(
    grad_ref, mine_ref, other_ref, fwd_ref, rim_ref, send_rows_ref, lift_ref, send_ref
):
    core = lax.axis_index("corner")
    freqs = grad_ref.shape[0] // 2
    margin = rim_ref.shape[2]
    tile = fwd_ref.shape[1] - 2 * margin
    last = tile + margin

    def both(values):
        low_re = values[:freqs]
        low_im = values[freqs:]
        upper = jnp.concatenate([low_re, low_im], axis=1)
        lower = jnp.concatenate([low_im, -low_re], axis=1)
        return jnp.concatenate([upper, lower], axis=0)

    mine = mine_ref[...]
    other = other_ref[...]
    before = both(by_core(core, mine, other))
    here = both(grad_ref[...])
    after = both(by_core(core, other, mine))
    middle = dot(here, fwd_ref[:, margin : margin + tile])
    lift_ref[:, :margin] = (middle[:, :margin] + dot(before, fwd_ref[:, last:])).astype(
        jnp.bfloat16
    )
    lift_ref[:, tile - margin : tile] = (
        middle[:, tile - margin :] + dot(after, fwd_ref[:, :margin])
    ).astype(jnp.bfloat16)
    lift_ref[:, tile:] = (
        dot(before, rim_ref[0]) + dot(here, rim_ref[1]) + dot(after, rim_ref[2])
    ).astype(jnp.bfloat16)
    send_ref[...] = dot(send_rows_ref[core], lift_ref[...]).astype(jnp.bfloat16)


def frame_kernel(
    lift_ref, own_rows_ref, level_ref, above_ref, below_ref, left_ref, right_ref,
    grad_ref, frame_ref, slope_ref,
):
    core = lax.axis_index("corner")
    tile = level_ref.shape[0]
    margin = above_ref.shape[0]
    rows = lift_ref.shape[0]
    grad_ref[...] = dot(own_rows_ref[...], lift_ref[...])
    mine = above_ref[...].astype(jnp.float32)
    other = below_ref[...].astype(jnp.float32)
    above = by_core(core, mine, other)
    below = by_core(core, other, mine)
    frame_ref[:tile, :tile] = level_ref[...].astype(jnp.float32) * 0.125
    frame_ref[tile:, :tile] = jnp.where(
        lax.broadcasted_iota(jnp.int32, (RIM, tile), 0) < RIM // 2,
        below[:RIM],
        above[margin - RIM :],
    )
    at = lax.broadcasted_iota(jnp.int32, (RIM, margin), 0)
    lane = lax.broadcasted_iota(jnp.int32, (RIM, margin), 1)
    place_left = ((lane == margin - LS_STEPS + at) & (at < LS_STEPS)).astype(jnp.bfloat16)
    place_right = ((lane == at) & (at < LS_STEPS)).astype(jnp.bfloat16)
    for block in range(tile // margin + 1):
        part = slice(rows + block * RIM, rows + (block + 1) * RIM)
        left = by_core(core, left_ref[part, :], right_ref[part, :])
        right = by_core(core, right_ref[part, :], left_ref[part, :])
        placed = dot_general(left, place_left, 0, 0) + dot_general(right, place_right, 0, 0)
        size = margin if block < tile // margin else RIM
        frame_ref[block * margin : block * margin + size, tile:] = placed[:size]
    trans = jnp.tanh(0.25 * frame_ref[...])
    slope_ref[...] = 0.25 * (1.0 - trans * trans)


def advance_kernel(extent, grad_ref, mine_ref, other_ref, frame_ref, slope_ref, out_ref):
    core = lax.axis_index("corner")
    tile = out_ref.shape[0]
    rows, cols = frame_ref.shape
    margin = cols - tile
    mine = mine_ref[...].astype(jnp.float32)
    other = other_ref[...].astype(jnp.float32)
    before = by_core(core, mine, other)
    after = by_core(core, other, mine)
    grad = grad_ref[...] + jnp.concatenate(
        [before[:margin], after[:margin], before[margin:] + after[margin:]], axis=0
    )
    speed = SPEED_GAIN * (grad * slope_ref[...])

    def inside(axis, dim, size, count):
        at = lax.broadcasted_iota(jnp.int32, (rows, cols), dim)
        index = lax.axis_index(axis)
        behind = (at >= tile + LS_STEPS) & (index > 0)
        ahead = (at >= tile) & (at < tile + LS_STEPS) & (index < count - 1)
        return (at < tile) | behind | ahead

    keep = inside("ty", 0, rows, extent[0]) & inside("tx", 1, cols, extent[1])
    level = frame_ref[...]
    for _ in range(LS_STEPS):
        up = pltpu.roll(level, 1, 0)
        down = pltpu.roll(level, rows - 1, 0)
        left = pltpu.roll(level, 1, 1)
        right = pltpu.roll(level, cols - 1, 1)
        slope_y = 0.5 * (down - up)
        slope_x = 0.5 * (right - left)
        spread = up + down + left + right - 4.0 * level
        level = (
            level
            - speed * jnp.sqrt(GRAD_FLOOR + slope_y * slope_y + slope_x * slope_x)
            + SMOOTHING * spread
        )
        level = jnp.where(keep, level, 0.0)
    out_ref[...] = level[:tile, :tile]


def call(kernel, out_shape, *args, scratch=(), smem=0, name=None):
    vmem = pl.BlockSpec(memory_space=pltpu.VMEM)
    in_specs = [pl.BlockSpec(memory_space=pltpu.SMEM)] * smem + [vmem] * (len(args) - smem)
    return pl.pallas_call(
        kernel,
        out_shape=[jax.ShapeDtypeStruct(*item) for item in out_shape],
        in_specs=in_specs,
        out_specs=[vmem] * len(out_shape),
        scratch_shapes=list(scratch),
        compiler_params=pltpu.CompilerParams(vmem_limit_bytes=24 << 20),
        name=name,
    )(*args)


def along(axis, values):
    count = lax.axis_size(axis)
    pairs = []
    for index in range(count - 1):
        pairs.append((index * 2, (index + 1) * 2))
        pairs.append(((index + 1) * 2 + 1, index * 2 + 1))
    return lax.ppermute(values, (axis, "corner"), pairs)


def across(values):
    return lax.ppermute(values, "corner", [(0, 1), (1, 0)])


def body(level_init, target, kernels, corner_doses):
    tile = level_init.shape[0]
    margin = HALO
    freqs = KF
    count = kernels.shape[1]
    tables = make_tables(tile, margin, freqs)
    core = lax.axis_index("corner")
    bf16, f32 = jnp.bfloat16, jnp.float32
    extent = (lax.axis_size("ty"), lax.axis_size("tx"))

    edge = lax.dynamic_slice_in_dim(level_init, (1 - core) * (tile - margin), margin, axis=0)
    rows_mine = along("ty", (edge.astype(f32) * 0.125).astype(bf16))
    rows_other = across(rows_mine)
    strip_rows = (tile // margin + 1) * RIM
    lift, send = call(
        lift_kernel,
        [((2 * freqs, tile), bf16), ((2 * freqs + strip_rows, margin), bf16)],
        level_init, rows_mine, rows_other, tables["fwd"],
        name="lift",
    )
    cols_mine = along("tx", send)
    cols_other = across(cols_mine)
    resist, grad = call(
        corner_kernel,
        [((tile, tile), f32), ((2 * freqs, freqs), f32)],
        corner_doses, lift, cols_mine, cols_other, kernels[0], target,
        tables["fwd_t"], tables["inv"], tables["inv_t"],
        smem=1,
        scratch=[
            pltpu.VMEM((2 * freqs, count * freqs), bf16),
            pltpu.VMEM((2 * tile, count * freqs), bf16),
            pltpu.VMEM((count, tile, 2 * tile), f32),
            pltpu.VMEM((2 * tile, count * freqs), bf16),
        ],
        name="corner",
    )
    grad = (grad + across(grad)).astype(bf16)
    grad_mine = along("tx", grad)
    grad_other = across(grad_mine)
    grad_lift, piece = call(
        lift_grad_kernel,
        [((2 * freqs, tile + margin), bf16), ((margin + RIM, tile + margin), bf16)],
        grad, grad_mine, grad_other, tables["fwd"], tables["rim_cols"], tables["send_rows"],
        name="lift_grad",
    )
    piece_mine = along("ty", piece)
    piece_other = across(piece_mine)
    framed = (tile + RIM, tile + margin)
    own, frame, slope = call(
        frame_kernel,
        [(framed, f32)] * 3,
        grad_lift, tables["own_rows"], level_init, rows_mine, rows_other, cols_mine, cols_other,
        name="frame",
    )
    (level,) = call(
        functools.partial(advance_kernel, extent),
        [((tile, tile), f32)],
        own, piece_mine, piece_other, frame, slope,
        name="advance",
    )
    return (resist[None], level)


def solution(mesh):
    in_specs = (P("ty", "tx"), P("ty", "tx"), P("corner", None, None, None, None), P("corner"))
    out_specs = (P("corner", "ty", "tx"), P("ty", "tx"))
    return jax.shard_map(body, mesh=mesh, in_specs=in_specs, out_specs=out_specs, check_vma=False)
```

```python
import functools
import math

import jax
import jax.numpy as jnp
import numpy as np
from jax import lax
from jax.experimental import pallas as pl
from jax.experimental.pallas import tpu as pltpu
from jax.sharding import PartitionSpec as P

HALO = 128
KF = 128
LS_STEPS = 3

STEEPNESS = 4.0
THRESHOLD = 1.0
SPEED_GAIN = 4.0
SMOOTHING = 0.24
GRAD_FLOOR = 0.25

RIM = 16
PAD = 8


def make_tables(tile, margin, freqs):
    window = tile + 2 * margin
    shifts = np.arange(freqs) - freqs // 2
    places = np.arange(window)
    angles = 2.0 * math.pi / window * (shifts[:, None] * places[None, :] % window)
    scaled = 1.0 / math.sqrt(window)
    cos = np.cos(angles) * scaled
    sin = np.sin(angles) * scaled
    stacked = np.concatenate([cos, -sin], axis=0)
    inv_cos = cos[:, margin : margin + tile].T
    inv_sin = sin[:, margin : margin + tile].T
    inverse = np.block([[inv_cos, -inv_sin], [inv_sin, inv_cos]])

    def rim(width, offset):
        out = np.zeros((2 * freqs, width))
        for step in range(LS_STEPS):
            for place, at in ((tile + step, step), (step - LS_STEPS, width - LS_STEPS + step)):
                if 0 <= place + offset < window:
                    out[:, at] = stacked[:, place + offset]
        return out

    offsets = (margin + tile, margin, margin - tile)
    rim_cols = np.stack([rim(margin, offset) for offset in offsets])
    rim_rows = [rim(RIM, offset).T for offset in offsets]
    own_rows = np.concatenate([stacked[:, margin : margin + tile].T, rim_rows[1]])
    send_rows = np.stack(
        [
            np.concatenate([stacked[:, :margin].T, rim_rows[2]]),
            np.concatenate([stacked[:, tile + margin :].T, rim_rows[0]]),
        ]
    )
    as_const = lambda values: np.asarray(values, np.float32).astype(jnp.bfloat16)
    return {
        "fwd": as_const(stacked),
        "fwd_t": as_const(stacked.T),
        "inv": as_const(inverse),
        "inv_t": as_const(inverse.T),
        "rim_cols": as_const(rim_cols),
        "own_rows": as_const(own_rows),
        "send_rows": as_const(send_rows),
    }


def dot(left, right):
    return jnp.dot(left, right, preferred_element_type=jnp.float32)


def dot_general(left, right, left_dim, right_dim):
    return lax.dot_general(
        left, right, (((left_dim,), (right_dim,)), ((), ())), preferred_element_type=jnp.float32
    )


def by_core(core, first, second):
    return jnp.where(core == 0, first, second)


def lift_kernel(level_ref, mine_ref, other_ref, fwd_ref, lift_ref, send_ref):
    core = lax.axis_index("corner")
    tile = level_ref.shape[0]
    margin = mine_ref.shape[0]
    level = level_ref[...].astype(jnp.float32) * 0.125
    mine = mine_ref[...].astype(jnp.float32)
    other = other_ref[...].astype(jnp.float32)
    above = by_core(core, mine, other)
    below = by_core(core, other, mine)
    squash = lambda values: jnp.tanh(0.25 * values).astype(jnp.bfloat16)
    lift = (
        dot(fwd_ref[:, :margin], squash(above))
        + dot(fwd_ref[:, margin : margin + tile], squash(level))
        + dot(fwd_ref[:, margin + tile :], squash(below))
    ).astype(jnp.bfloat16)
    lift_ref[...] = lift
    rows = lift.shape[0]
    send_ref[:rows, :] = by_core(core, lift[:, :margin], lift[:, tile - margin :])
    at = lax.broadcasted_iota(jnp.int32, (RIM, margin), 0)
    lane = lax.broadcasted_iota(jnp.int32, (RIM, margin), 1)
    first = by_core(core, 0, margin - LS_STEPS)
    pick = ((lane == first + at) & (at < LS_STEPS)).astype(jnp.bfloat16)
    rim = jnp.where(
        lax.broadcasted_iota(jnp.int32, (RIM, tile), 0) < RIM // 2,
        below[:RIM],
        above[margin - RIM :],
    )
    strip = by_core(core, level[:, :margin], level[:, tile - margin :]).astype(jnp.bfloat16)
    rim_strip = by_core(core, rim[:, :margin], rim[:, tile - margin :]).astype(jnp.bfloat16)
    for block in range(tile // margin):
        picked = dot_general(pick, strip[block * margin : (block + 1) * margin], 1, 1)
        send_ref[rows + block * RIM : rows + (block + 1) * RIM, :] = picked.astype(jnp.bfloat16)
    padded = jnp.concatenate([rim_strip, jnp.zeros((margin - RIM, margin), jnp.bfloat16)], axis=0)
    block = tile // margin
    send_ref[rows + block * RIM : rows + (block + 1) * RIM, :] = dot_general(
        pick, padded, 1, 1
    ).astype(jnp.bfloat16)


def corner_kernel(
    dose_ref,
    lift_ref,
    mine_ref,
    other_ref,
    kernels_ref,
    target_ref,
    fwd_t_ref,
    inv_ref,
    inv_t_ref,
    resist_ref,
    grad_ref,
    blur_ref,
    proj_ref,
    field_ref,
    back_ref,
):
    core = lax.axis_index("corner")
    tile = target_ref.shape[0]
    rows = lift_ref.shape[0]
    freqs = rows // 2
    margin = mine_ref.shape[1]
    count = kernels_ref.shape[0]
    mine = mine_ref[:rows, :]
    other = other_ref[:rows, :]
    mixed = (
        dot(by_core(core, mine, other), fwd_t_ref[:margin, :])
        + dot(lift_ref[...], fwd_t_ref[margin : margin + tile, :])
        + dot(by_core(core, other, mine), fwd_t_ref[margin + tile :, :])
    )
    spec_re = mixed[:freqs, :freqs] - mixed[freqs:, freqs:]
    spec_im = mixed[:freqs, freqs:] + mixed[freqs:, :freqs]
    for g in range(count):
        kernel_re = kernels_ref[g, 0]
        kernel_im = kernels_ref[g, 1]
        cols = slice(g * freqs, (g + 1) * freqs)
        blur_ref[:freqs, cols] = (kernel_re * spec_re - kernel_im * spec_im).astype(jnp.bfloat16)
        blur_ref[freqs:, cols] = (kernel_re * spec_im + kernel_im * spec_re).astype(jnp.bfloat16)
    proj_ref[...] = dot(inv_ref[...], blur_ref[...]).astype(jnp.bfloat16)
    power = jnp.zeros((tile, tile), jnp.float32)
    for g in range(count):
        cols = slice(g * freqs, (g + 1) * freqs)
        pair = jnp.concatenate([proj_ref[:tile, cols], proj_ref[tile:, cols]], axis=1)
        field = dot(pair, inv_t_ref[...])
        field_ref[g] = field
        power = power + (field[:, :tile] * field[:, :tile] + field[:, tile:] * field[:, tile:])
    dose = dose_ref[0]
    resist = jax.nn.sigmoid(STEEPNESS * (dose * power - THRESHOLD))
    resist_ref[...] = resist
    goal = target_ref[...].astype(jnp.float32)
    sens = 2.0 * (resist - goal) * STEEPNESS * dose * resist * (1.0 - resist)
    twice = 2.0 * sens
    twice = jnp.concatenate([twice, twice], axis=1)
    for g in range(count):
        cols = slice(g * freqs, (g + 1) * freqs)
        back = dot((twice * field_ref[g]).astype(jnp.bfloat16), inv_ref[...]).astype(jnp.bfloat16)
        back_ref[:tile, cols] = back[:, :freqs]
        back_ref[tile:, cols] = back[:, freqs:]
    blurred = dot(inv_t_ref[...], back_ref[...])
    grad_re = jnp.zeros((freqs, freqs), jnp.float32)
    grad_im = jnp.zeros((freqs, freqs), jnp.float32)
    for g in range(count):
        kernel_re = kernels_ref[g, 0]
        kernel_im = kernels_ref[g, 1]
        cols = slice(g * freqs, (g + 1) * freqs)
        blur_re = blurred[:freqs, cols]
        blur_im = blurred[freqs:, cols]
        grad_re = grad_re + (kernel_re * blur_re + kernel_im * blur_im)
        grad_im = grad_im + (kernel_re * blur_im - kernel_im * blur_re)
    grad_ref[:freqs, :] = grad_re
    grad_ref[freqs:, :] = grad_im


def lift_grad_kernel(
    grad_ref, mine_ref, other_ref, fwd_ref, rim_ref, send_rows_ref, lift_ref, send_ref
):
    core = lax.axis_index("corner")
    freqs = grad_ref.shape[0] // 2
    margin = rim_ref.shape[2]
    tile = fwd_ref.shape[1] - 2 * margin
    last = tile + margin

    def both(values):
        low_re = values[:freqs]
        low_im = values[freqs:]
        upper = jnp.concatenate([low_re, low_im], axis=1)
        lower = jnp.concatenate([low_im, -low_re], axis=1)
        return jnp.concatenate([upper, lower], axis=0)

    mine = mine_ref[...]
    other = other_ref[...]
    before = both(by_core(core, mine, other))
    here = both(grad_ref[...])
    after = both(by_core(core, other, mine))
    middle = dot(here, fwd_ref[:, margin : margin + tile])
    lift_ref[:, :margin] = (middle[:, :margin] + dot(before, fwd_ref[:, last:])).astype(
        jnp.bfloat16
    )
    lift_ref[:, tile - margin : tile] = (
        middle[:, tile - margin :] + dot(after, fwd_ref[:, :margin])
    ).astype(jnp.bfloat16)
    lift_ref[:, tile:] = (
        dot(before, rim_ref[0]) + dot(here, rim_ref[1]) + dot(after, rim_ref[2])
    ).astype(jnp.bfloat16)
    send_ref[...] = dot(send_rows_ref[core], lift_ref[...]).astype(jnp.bfloat16)


def frame_kernel(
    lift_ref, own_rows_ref, level_ref, above_ref, below_ref, left_ref, right_ref,
    grad_ref, frame_ref, slope_ref,
):
    core = lax.axis_index("corner")
    tile = level_ref.shape[0]
    margin = above_ref.shape[0]
    rows = lift_ref.shape[0]
    grad_ref[...] = dot(own_rows_ref[...], lift_ref[...])
    mine = above_ref[...].astype(jnp.float32)
    other = below_ref[...].astype(jnp.float32)
    frame_ref[:PAD, :tile] = 0.5 * by_core(core, mine, other)[margin - PAD :]
    frame_ref[PAD : PAD + tile, :tile] = level_ref[...].astype(jnp.float32) * 0.0625
    frame_ref[PAD + tile :, :tile] = 0.5 * by_core(core, other, mine)[:PAD]
    at = lax.broadcasted_iota(jnp.int32, (RIM, margin), 0)
    lane = lax.broadcasted_iota(jnp.int32, (RIM, margin), 1)
    place_left = ((lane == margin - LS_STEPS + at) & (at < LS_STEPS)).astype(jnp.bfloat16)
    place_right = ((lane == at) & (at < LS_STEPS)).astype(jnp.bfloat16)
    for block in range(tile // margin + 1):
        part = slice(rows + block * RIM, rows + (block + 1) * RIM)
        left = by_core(core, left_ref[part, :], right_ref[part, :])
        right = by_core(core, right_ref[part, :], left_ref[part, :])
        placed = dot_general(left, place_left, 0, 0) + dot_general(right, place_right, 0, 0)
        placed = 0.5 * placed
        if block < tile // margin:
            start = PAD + block * margin
            frame_ref[start : start + margin, tile:] = placed
        else:
            frame_ref[PAD + tile :, tile:] = placed[:PAD]
            frame_ref[:PAD, tile:] = placed[PAD:RIM]
    trans = jnp.tanh(0.5 * frame_ref[...])
    slope_ref[...] = (SPEED_GAIN * 0.5 * 0.25) * (1.0 - trans * trans)


def advance_kernel(
    extent, grad_ref, mine_ref, other_ref, frame_ref, slope_ref, out_ref, speed_ref, *level_refs
):
    core = lax.axis_index("corner")
    tile = out_ref.shape[0]
    rows, cols = frame_ref.shape
    margin = cols - tile
    blocks = cols // margin
    first, last = level_refs[:blocks], level_refs[blocks:]

    lane = lax.broadcasted_iota(jnp.int32, (PAD, margin), 1)
    at_ty, at_tx = lax.axis_index("ty"), lax.axis_index("tx")
    all_lanes = lane >= 0
    keep_above = all_lanes & (at_ty > 0)
    keep_below = all_lanes & (at_ty < extent[0] - 1)
    keep_cols = ((lane >= margin // 2) & (at_tx > 0)) | (
        (lane < margin // 2) & (at_tx < extent[1] - 1)
    )

    before = by_core(core, mine_ref[...].astype(jnp.float32), other_ref[...].astype(jnp.float32))
    after = by_core(core, other_ref[...].astype(jnp.float32), mine_ref[...].astype(jnp.float32))
    rim = before[margin:] + after[margin:] + grad_ref[tile:]
    speed_ref[:PAD] = rim[PAD:] * slope_ref[:PAD]
    speed_ref[PAD + tile :] = rim[:PAD] * slope_ref[PAD + tile :]
    for half, part in ((0, before), (1, after)):
        at = half * margin
        speed_ref[PAD + at : PAD + at + margin] = (
            grad_ref[at : at + margin] + part[:margin]
        ) * slope_ref[PAD + at : PAD + at + margin]
    for ref in level_refs:
        ref[:PAD] = jnp.zeros((PAD, margin), jnp.float32)
        ref[PAD + rows :] = jnp.zeros((PAD, margin), jnp.float32)
    for block in range(blocks):
        first[block][PAD : PAD + rows] = frame_ref[:, block * margin : (block + 1) * margin]

    source, target = first, last
    for step in range(LS_STEPS):
        final = step == LS_STEPS - 1
        for at in range(PAD if final else 0, rows - PAD if final else rows, PAD):
            here = [ref[PAD + at : 2 * PAD + at] for ref in source]
            back = [pltpu.roll(part, 1, 1) for part in here]
            ahead = [pltpu.roll(part, margin - 1, 1) for part in here]
            for block in range(blocks - 1 if final else blocks):
                up = source[block][PAD + at - 1 : 2 * PAD + at - 1]
                down = source[block][PAD + at + 1 : 2 * PAD + at + 1]
                left = jnp.where(lane == 0, back[block - 1], back[block])
                right = jnp.where(lane == margin - 1, ahead[(block + 1) % blocks], ahead[block])
                slope_y = down - up
                slope_x = right - left
                square = GRAD_FLOOR + slope_y * slope_y + slope_x * slope_x
                level = (
                    (1.0 - 4.0 * SMOOTHING) * here[block]
                    + SMOOTHING * ((up + down) + (left + right))
                    - speed_ref[at : at + PAD, block * margin : (block + 1) * margin]
                    * (square * lax.rsqrt(square))
                )
                if final:
                    out_ref[at - PAD : at, block * margin : (block + 1) * margin] = 2.0 * level
                    continue
                if at == 0:
                    level = jnp.where(keep_above, level, 0.0)
                if at == rows - PAD:
                    level = jnp.where(keep_below, level, 0.0)
                if block == blocks - 1:
                    level = jnp.where(keep_cols, level, 0.0)
                target[block][PAD + at : 2 * PAD + at] = level
        source, target = target, source


def load_kernel(*refs):
    count = len(refs) // 2
    sems = refs[-1]
    copies = [
        pltpu.make_async_copy(refs[i], refs[count + i], sems.at[i]) for i in range(count)
    ]
    for copy in copies:
        copy.start()
    for copy in copies:
        copy.wait()


def load(*arrays):
    return pl.pallas_call(
        load_kernel,
        out_shape=[jax.ShapeDtypeStruct(item.shape, item.dtype) for item in arrays],
        in_specs=[pl.BlockSpec(memory_space=pltpu.HBM)] * len(arrays),
        out_specs=[pl.BlockSpec(memory_space=pltpu.VMEM)] * len(arrays),
        scratch_shapes=[pltpu.SemaphoreType.DMA((len(arrays),))],
        compiler_params=pltpu.CompilerParams(vmem_limit_bytes=24 << 20),
        cost_estimate=pl.CostEstimate(flops=0, bytes_accessed=8 << 20, transcendentals=0),
        name="load",
    )(*[pltpu.with_memory_space_constraint(item, pltpu.HBM) for item in arrays])


def call(kernel, out_shape, *args, scratch=(), smem=0):
    vmem = pl.BlockSpec(memory_space=pltpu.VMEM)
    in_specs = [pl.BlockSpec(memory_space=pltpu.SMEM)] * smem + [vmem] * (len(args) - smem)
    return pl.pallas_call(
        kernel,
        out_shape=[jax.ShapeDtypeStruct(*item) for item in out_shape],
        in_specs=in_specs,
        out_specs=[vmem] * len(out_shape),
        scratch_shapes=list(scratch),
        compiler_params=pltpu.CompilerParams(vmem_limit_bytes=24 << 20),
    )(*args)


def along(axis, values):
    count = lax.axis_size(axis)
    pairs = []
    for index in range(count - 1):
        pairs.append((index * 2 + 1, (index + 1) * 2))
        pairs.append(((index + 1) * 2, index * 2 + 1))
    return lax.ppermute(values, (axis, "corner"), pairs)


def across(values):
    return lax.ppermute(values, "corner", [(0, 1), (1, 0)])


def step(level_init, target, kernels, corner_doses):
    tile = level_init.shape[0]
    margin = HALO
    freqs = KF
    count = kernels.shape[1]
    tables = make_tables(tile, margin, freqs)
    core = lax.axis_index("corner")
    bf16, f32 = jnp.bfloat16, jnp.float32
    extent = (lax.axis_size("ty"), lax.axis_size("tx"))

    edge = lax.dynamic_slice_in_dim(level_init, core * (tile - margin), margin, axis=0)
    edge = (edge.astype(f32) * 0.125).astype(bf16)
    rows_mine = along("ty", edge)
    rows_other = across(rows_mine)
    names = sorted(tables)
    level_init, target, kernels, *loaded = load(
        level_init, target, kernels[0], *(tables[name] for name in names)
    )
    tables = dict(zip(names, loaded))
    strip_rows = (tile // margin + 1) * RIM
    lift, send = call(
        lift_kernel,
        [((2 * freqs, tile), bf16), ((2 * freqs + strip_rows, margin), bf16)],
        level_init, rows_mine, rows_other, tables["fwd"],
    )
    cols_mine = along("tx", send)
    cols_other = across(cols_mine)
    resist, grad = call(
        corner_kernel,
        [((tile, tile), f32), ((2 * freqs, freqs), f32)],
        corner_doses, lift, cols_mine, cols_other, kernels, target,
        tables["fwd_t"], tables["inv"], tables["inv_t"],
        smem=1,
        scratch=[
            pltpu.VMEM((2 * freqs, count * freqs), bf16),
            pltpu.VMEM((2 * tile, count * freqs), bf16),
            pltpu.VMEM((count, tile, 2 * tile), f32),
            pltpu.VMEM((2 * tile, count * freqs), bf16),
        ],
    )
    grad = (grad + across(grad)).astype(bf16)
    grad_mine = along("tx", grad)
    grad_other = across(grad_mine)
    grad_lift, piece = call(
        lift_grad_kernel,
        [((2 * freqs, tile + margin), bf16), ((margin + RIM, tile + margin), bf16)],
        grad, grad_mine, grad_other, tables["fwd"], tables["rim_cols"], tables["send_rows"],
    )
    piece_mine = along("ty", piece)
    piece_other = across(piece_mine)
    framed = (tile + RIM, tile + margin)
    own, frame, slope = call(
        frame_kernel,
        [(framed, f32)] * 3,
        grad_lift, tables["own_rows"], level_init, rows_mine, rows_other, cols_mine, cols_other,
    )
    (level,) = call(
        functools.partial(advance_kernel, extent),
        [((tile, tile), f32)],
        own, piece_mine, piece_other, frame, slope,
        scratch=[pltpu.VMEM(framed, f32)]
        + [pltpu.VMEM((framed[0] + 2 * PAD, margin), f32)] * (2 * framed[1] // margin),
    )
    return (resist[None], level)


def solution(mesh):
    in_specs = (P("ty", "tx"), P("ty", "tx"), P("corner", None, None, None, None), P("corner"))
    out_specs = (P("corner", "ty", "tx"), P("ty", "tx"))
    return jax.shard_map(step, mesh=mesh, in_specs=in_specs, out_specs=out_specs, check_vma=False)
```

```python
import functools
import math

import jax
import jax.numpy as jnp
import numpy as np
from jax import lax
from jax.experimental import pallas as pl
from jax.experimental.pallas import tpu as pltpu
from jax.sharding import PartitionSpec as P

HALO = 128
KF = 128
LS_STEPS = 3

STEEPNESS = 4.0
THRESHOLD = 1.0
SPEED_GAIN = 4.0
SMOOTHING = 0.24
GRAD_FLOOR = 0.25

RIM = 16
PAD = 8


def make_tables(tile, margin, freqs):
    window = tile + 2 * margin
    shifts = np.arange(freqs) - freqs // 2
    places = np.arange(window)
    angles = 2.0 * math.pi / window * (shifts[:, None] * places[None, :] % window)
    scaled = 1.0 / math.sqrt(window)
    cos = np.cos(angles) * scaled
    sin = np.sin(angles) * scaled
    stacked = np.concatenate([cos, -sin], axis=0)
    inv_cos = cos[:, margin : margin + tile].T
    inv_sin = sin[:, margin : margin + tile].T
    inverse = np.block([[inv_cos, -inv_sin], [inv_sin, inv_cos]])

    def rim(width, offset):
        out = np.zeros((2 * freqs, width))
        for step in range(LS_STEPS):
            for place, at in ((tile + step, step), (step - LS_STEPS, width - LS_STEPS + step)):
                if 0 <= place + offset < window:
                    out[:, at] = stacked[:, place + offset]
        return out

    offsets = (margin + tile, margin, margin - tile)
    rim_cols = np.stack([rim(margin, offset) for offset in offsets])
    rim_rows = [rim(RIM, offset).T for offset in offsets]
    own_rows = np.concatenate([stacked[:, margin : margin + tile].T, rim_rows[1]])
    send_rows = np.stack(
        [
            np.concatenate([stacked[:, :margin].T, rim_rows[2]]),
            np.concatenate([stacked[:, tile + margin :].T, rim_rows[0]]),
        ]
    )
    as_const = lambda values: np.asarray(values, np.float32).astype(jnp.bfloat16)
    return {
        "fwd": as_const(stacked),
        "fwd_t": as_const(stacked.T),
        "inv": as_const(inverse),
        "inv_t": as_const(inverse.T),
        "rim_cols": as_const(rim_cols),
        "own_rows": as_const(own_rows),
        "send_rows": as_const(send_rows),
    }


def dot(left, right):
    return jnp.dot(left, right, preferred_element_type=jnp.float32)


def dot_general(left, right, left_dim, right_dim):
    return lax.dot_general(
        left, right, (((left_dim,), (right_dim,)), ((), ())), preferred_element_type=jnp.float32
    )


def by_core(core, first, second):
    return jnp.where(core == 0, first, second)


def lift_kernel(counts, level_ref, mine_ref, other_ref, fwd_ref, lift_ref, send_ref):
    core = lax.axis_index("corner")
    tile = level_ref.shape[0]
    margin = mine_ref.shape[0]
    level = level_ref[...].astype(jnp.float32) * 0.125
    above, below = ordered("ty", counts, mine_ref[...], other_ref[...])
    above = above.astype(jnp.float32)
    below = below.astype(jnp.float32)
    squash = lambda values: jnp.tanh(0.25 * values).astype(jnp.bfloat16)
    lift = (
        dot(fwd_ref[:, :margin], squash(above))
        + dot(fwd_ref[:, margin : margin + tile], squash(level))
        + dot(fwd_ref[:, margin + tile :], squash(below))
    ).astype(jnp.bfloat16)
    lift_ref[...] = lift
    rows = lift.shape[0]
    send_ref[:rows, :] = by_core(core, lift[:, :margin], lift[:, tile - margin :])
    at = lax.broadcasted_iota(jnp.int32, (RIM, margin), 0)
    lane = lax.broadcasted_iota(jnp.int32, (RIM, margin), 1)
    first = by_core(core, 0, margin - LS_STEPS)
    pick = ((lane == first + at) & (at < LS_STEPS)).astype(jnp.bfloat16)
    rim = jnp.where(
        lax.broadcasted_iota(jnp.int32, (RIM, tile), 0) < RIM // 2,
        below[:RIM],
        above[margin - RIM :],
    )
    strip = by_core(core, level[:, :margin], level[:, tile - margin :]).astype(jnp.bfloat16)
    rim_strip = by_core(core, rim[:, :margin], rim[:, tile - margin :]).astype(jnp.bfloat16)
    for block in range(tile // margin):
        picked = dot_general(pick, strip[block * margin : (block + 1) * margin], 1, 1)
        send_ref[rows + block * RIM : rows + (block + 1) * RIM, :] = picked.astype(jnp.bfloat16)
    padded = jnp.concatenate([rim_strip, jnp.zeros((margin - RIM, margin), jnp.bfloat16)], axis=0)
    block = tile // margin
    send_ref[rows + block * RIM : rows + (block + 1) * RIM, :] = dot_general(
        pick, padded, 1, 1
    ).astype(jnp.bfloat16)


def corner_kernel(
    counts,
    dose_ref,
    lift_ref,
    mine_ref,
    other_ref,
    kernels_ref,
    target_ref,
    fwd_t_ref,
    inv_ref,
    inv_t_ref,
    resist_ref,
    grad_ref,
    blur_ref,
    proj_ref,
    field_ref,
    back_ref,
):
    tile = target_ref.shape[0]
    rows = lift_ref.shape[0]
    freqs = rows // 2
    margin = mine_ref.shape[1]
    count = kernels_ref.shape[0]
    left, right = ordered("tx", counts, mine_ref[:rows, :], other_ref[:rows, :])
    mixed = (
        dot(left, fwd_t_ref[:margin, :])
        + dot(lift_ref[...], fwd_t_ref[margin : margin + tile, :])
        + dot(right, fwd_t_ref[margin + tile :, :])
    )
    spec_re = mixed[:freqs, :freqs] - mixed[freqs:, freqs:]
    spec_im = mixed[:freqs, freqs:] + mixed[freqs:, :freqs]
    for g in range(count):
        kernel_re = kernels_ref[g, 0]
        kernel_im = kernels_ref[g, 1]
        cols = slice(g * freqs, (g + 1) * freqs)
        blur_ref[:freqs, cols] = (kernel_re * spec_re - kernel_im * spec_im).astype(jnp.bfloat16)
        blur_ref[freqs:, cols] = (kernel_re * spec_im + kernel_im * spec_re).astype(jnp.bfloat16)
    proj_ref[...] = dot(inv_ref[...], blur_ref[...]).astype(jnp.bfloat16)
    power = jnp.zeros((tile, tile), jnp.float32)
    for g in range(count):
        cols = slice(g * freqs, (g + 1) * freqs)
        pair = jnp.concatenate([proj_ref[:tile, cols], proj_ref[tile:, cols]], axis=1)
        field = dot(pair, inv_t_ref[...])
        field_ref[g] = field
        power = power + (field[:, :tile] * field[:, :tile] + field[:, tile:] * field[:, tile:])
    dose = dose_ref[0]
    resist = jax.nn.sigmoid(STEEPNESS * (dose * power - THRESHOLD))
    resist_ref[...] = resist
    goal = target_ref[...].astype(jnp.float32)
    sens = 2.0 * (resist - goal) * STEEPNESS * dose * resist * (1.0 - resist)
    twice = 2.0 * sens
    twice = jnp.concatenate([twice, twice], axis=1)
    for g in range(count):
        cols = slice(g * freqs, (g + 1) * freqs)
        back = dot((twice * field_ref[g]).astype(jnp.bfloat16), inv_ref[...]).astype(jnp.bfloat16)
        back_ref[:tile, cols] = back[:, :freqs]
        back_ref[tile:, cols] = back[:, freqs:]
    blurred = dot(inv_t_ref[...], back_ref[...])
    grad_re = jnp.zeros((freqs, freqs), jnp.float32)
    grad_im = jnp.zeros((freqs, freqs), jnp.float32)
    for g in range(count):
        kernel_re = kernels_ref[g, 0]
        kernel_im = kernels_ref[g, 1]
        cols = slice(g * freqs, (g + 1) * freqs)
        blur_re = blurred[:freqs, cols]
        blur_im = blurred[freqs:, cols]
        grad_re = grad_re + (kernel_re * blur_re + kernel_im * blur_im)
        grad_im = grad_im + (kernel_re * blur_im - kernel_im * blur_re)
    grad_ref[:freqs, :] = grad_re
    grad_ref[freqs:, :] = grad_im


def lift_grad_kernel(
    counts,
    grad_ref, mine_ref, other_ref, fwd_ref, rim_ref, send_rows_ref, lift_ref, send_ref
):
    to_after = 1 - lax.rem(lax.axis_index("corner") + lax.axis_index("ty"), 2)
    freqs = grad_ref.shape[0] // 2
    margin = rim_ref.shape[2]
    tile = fwd_ref.shape[1] - 2 * margin
    last = tile + margin

    def both(values):
        low_re = values[:freqs]
        low_im = values[freqs:]
        upper = jnp.concatenate([low_re, low_im], axis=1)
        lower = jnp.concatenate([low_im, -low_re], axis=1)
        return jnp.concatenate([upper, lower], axis=0)

    before, after = ordered("tx", counts, mine_ref[...], other_ref[...])
    before = both(before)
    here = both(grad_ref[...])
    after = both(after)
    middle = dot(here, fwd_ref[:, margin : margin + tile])
    lift_ref[:, :margin] = (middle[:, :margin] + dot(before, fwd_ref[:, last:])).astype(
        jnp.bfloat16
    )
    lift_ref[:, tile - margin : tile] = (
        middle[:, tile - margin :] + dot(after, fwd_ref[:, :margin])
    ).astype(jnp.bfloat16)
    lift_ref[:, tile:] = (
        dot(before, rim_ref[0]) + dot(here, rim_ref[1]) + dot(after, rim_ref[2])
    ).astype(jnp.bfloat16)
    send_ref[...] = dot(send_rows_ref[to_after], lift_ref[...]).astype(jnp.bfloat16)


def frame_kernel(
    counts,
    lift_ref, own_rows_ref, level_ref, mine_ref, other_ref, cols_mine_ref, cols_other_ref,
    grad_ref, frame_ref, slope_ref,
):
    tile = level_ref.shape[0]
    margin = mine_ref.shape[0]
    rows = lift_ref.shape[0]
    grad_ref[...] = dot(own_rows_ref[...], lift_ref[...])
    above, below = ordered("ty", counts, mine_ref[...], other_ref[...])
    frame_ref[:PAD, :tile] = 0.5 * above.astype(jnp.float32)[margin - PAD :]
    frame_ref[PAD : PAD + tile, :tile] = level_ref[...].astype(jnp.float32) * 0.0625
    frame_ref[PAD + tile :, :tile] = 0.5 * below.astype(jnp.float32)[:PAD]
    at = lax.broadcasted_iota(jnp.int32, (RIM, margin), 0)
    lane = lax.broadcasted_iota(jnp.int32, (RIM, margin), 1)
    place_left = ((lane == margin - LS_STEPS + at) & (at < LS_STEPS)).astype(jnp.bfloat16)
    place_right = ((lane == at) & (at < LS_STEPS)).astype(jnp.bfloat16)
    for block in range(tile // margin + 1):
        part = slice(rows + block * RIM, rows + (block + 1) * RIM)
        left, right = ordered("tx", counts, cols_mine_ref[part, :], cols_other_ref[part, :])
        placed = dot_general(left, place_left, 0, 0) + dot_general(right, place_right, 0, 0)
        placed = 0.5 * placed
        if block < tile // margin:
            start = PAD + block * margin
            frame_ref[start : start + margin, tile:] = placed
        else:
            frame_ref[PAD + tile :, tile:] = placed[:PAD]
            frame_ref[:PAD, tile:] = placed[PAD:RIM]
    trans = jnp.tanh(0.5 * frame_ref[...])
    slope_ref[...] = (SPEED_GAIN * 0.5 * 0.25) * (1.0 - trans * trans)


def advance_kernel(
    counts, grad_ref, mine_ref, other_ref, frame_ref, slope_ref, out_ref, speed_ref, *level_refs
):
    tile = out_ref.shape[0]
    rows, cols = frame_ref.shape
    margin = cols - tile
    blocks = cols // margin
    first, last = level_refs[:blocks], level_refs[blocks:]

    lane = lax.broadcasted_iota(jnp.int32, (PAD, margin), 1)
    at_ty, at_tx = lax.axis_index("ty"), lax.axis_index("tx")
    all_lanes = lane >= 0
    keep_above = all_lanes & (at_ty > 0)
    keep_below = all_lanes & (at_ty < counts["ty"] - 1)
    keep_cols = ((lane >= margin // 2) & (at_tx > 0)) | (
        (lane < margin // 2) & (at_tx < counts["tx"] - 1)
    )

    before, after = ordered("ty", counts, mine_ref[...], other_ref[...])
    before = before.astype(jnp.float32)
    after = after.astype(jnp.float32)
    rim = before[margin:] + after[margin:] + grad_ref[tile:]
    speed_ref[:PAD] = rim[PAD:] * slope_ref[:PAD]
    speed_ref[PAD + tile :] = rim[:PAD] * slope_ref[PAD + tile :]
    for half, part in ((0, before), (1, after)):
        at = half * margin
        speed_ref[PAD + at : PAD + at + margin] = (
            grad_ref[at : at + margin] + part[:margin]
        ) * slope_ref[PAD + at : PAD + at + margin]
    for ref in level_refs:
        ref[:PAD] = jnp.zeros((PAD, margin), jnp.float32)
        ref[PAD + rows :] = jnp.zeros((PAD, margin), jnp.float32)
    for block in range(blocks):
        first[block][PAD : PAD + rows] = frame_ref[:, block * margin : (block + 1) * margin]

    source, target = first, last
    for step in range(LS_STEPS):
        final = step == LS_STEPS - 1
        for at in range(PAD if final else 0, rows - PAD if final else rows, PAD):
            here = [ref[PAD + at : 2 * PAD + at] for ref in source]
            back = [pltpu.roll(part, 1, 1) for part in here]
            ahead = [pltpu.roll(part, margin - 1, 1) for part in here]
            for block in range(blocks - 1 if final else blocks):
                up = source[block][PAD + at - 1 : 2 * PAD + at - 1]
                down = source[block][PAD + at + 1 : 2 * PAD + at + 1]
                left = jnp.where(lane == 0, back[block - 1], back[block])
                right = jnp.where(lane == margin - 1, ahead[(block + 1) % blocks], ahead[block])
                slope_y = down - up
                slope_x = right - left
                square = GRAD_FLOOR + slope_y * slope_y + slope_x * slope_x
                level = (
                    (1.0 - 4.0 * SMOOTHING) * here[block]
                    + SMOOTHING * ((up + down) + (left + right))
                    - speed_ref[at : at + PAD, block * margin : (block + 1) * margin]
                    * (square * lax.rsqrt(square))
                )
                if final:
                    out_ref[at - PAD : at, block * margin : (block + 1) * margin] = 2.0 * level
                    continue
                if at == 0:
                    level = jnp.where(keep_above, level, 0.0)
                if at == rows - PAD:
                    level = jnp.where(keep_below, level, 0.0)
                if block == blocks - 1:
                    level = jnp.where(keep_cols, level, 0.0)
                target[block][PAD + at : 2 * PAD + at] = level
        source, target = target, source


def load_kernel(*refs):
    count = len(refs) // 2
    sems = refs[-1]
    copies = [
        pltpu.make_async_copy(refs[i], refs[count + i], sems.at[i]) for i in range(count)
    ]
    for copy in copies:
        copy.start()
    for copy in copies:
        copy.wait()


def load(*arrays):
    return pl.pallas_call(
        load_kernel,
        out_shape=[jax.ShapeDtypeStruct(item.shape, item.dtype) for item in arrays],
        in_specs=[pl.BlockSpec(memory_space=pltpu.HBM)] * len(arrays),
        out_specs=[pl.BlockSpec(memory_space=pltpu.VMEM)] * len(arrays),
        scratch_shapes=[pltpu.SemaphoreType.DMA((len(arrays),))],
        compiler_params=pltpu.CompilerParams(vmem_limit_bytes=24 << 20),
        cost_estimate=pl.CostEstimate(flops=0, bytes_accessed=8 << 20, transcendentals=0),
        name="load",
    )(*[pltpu.with_memory_space_constraint(item, pltpu.HBM) for item in arrays])


def call(kernel, out_shape, *args, scratch=(), smem=0):
    vmem = pl.BlockSpec(memory_space=pltpu.VMEM)
    in_specs = [pl.BlockSpec(memory_space=pltpu.SMEM)] * smem + [vmem] * (len(args) - smem)
    return pl.pallas_call(
        kernel,
        out_shape=[jax.ShapeDtypeStruct(*item) for item in out_shape],
        in_specs=in_specs,
        out_specs=[vmem] * len(out_shape),
        scratch_shapes=list(scratch),
        compiler_params=pltpu.CompilerParams(vmem_limit_bytes=24 << 20),
    )(*args)


def along(axis, values):
    rows, cols = lax.axis_size("ty"), lax.axis_size("tx")
    count, others = (rows, cols) if axis == "ty" else (cols, rows)

    def device(place, other, core):
        row, col = (place, other) if axis == "ty" else (other, place)
        return (row * cols + col) * 2 + core

    pairs = []
    for other in range(others):
        free = {device(place, other, core) for place in (0, count - 1) for core in range(2)}
        for place in range(count - 1):
            cores = (place % 2, place % 2) if axis == "ty" else (1, 0)
            one, two = device(place, other, cores[0]), device(place + 1, other, cores[1])
            pairs += [(one, two), (two, one)]
            free -= {one, two}
        if other % 2 == 0 and other + 1 < others:
            step = device(0, 1, 0) - device(0, 0, 0)
            for one in sorted(free):
                pairs += [(one, one + step), (one + step, one)]
    return lax.ppermute(values, ("ty", "tx", "corner"), pairs)


def ordered(axis, counts, mine, other):
    index, core = lax.axis_index(axis), lax.axis_index("corner")
    count = counts[axis]
    from_before = (core != lax.rem(index, 2)) if axis == "ty" else core == 0
    before = jnp.where(from_before, mine, other)
    after = jnp.where(from_before, other, mine)
    zero = jnp.zeros_like(mine)
    return jnp.where(index > 0, before, zero), jnp.where(index < count - 1, after, zero)


def across(values):
    return lax.ppermute(values, "corner", [(0, 1), (1, 0)])


def step(level_init, target, kernels, corner_doses):
    tile = level_init.shape[0]
    margin = HALO
    freqs = KF
    count = kernels.shape[1]
    tables = make_tables(tile, margin, freqs)
    to_after = 1 - lax.rem(lax.axis_index("corner") + lax.axis_index("ty"), 2)
    bf16, f32 = jnp.bfloat16, jnp.float32
    counts = {"ty": lax.axis_size("ty"), "tx": lax.axis_size("tx")}

    edge = lax.dynamic_slice_in_dim(level_init, to_after * (tile - margin), margin, axis=0)
    edge = (edge.astype(f32) * 0.125).astype(bf16)
    rows_mine = along("ty", edge)
    rows_other = across(rows_mine)
    names = sorted(tables)
    level_init, target, kernels, *loaded = load(
        level_init, target, kernels[0], *(tables[name] for name in names)
    )
    tables = dict(zip(names, loaded))
    strip_rows = (tile // margin + 1) * RIM
    lift, send = call(
        functools.partial(lift_kernel, counts),
        [((2 * freqs, tile), bf16), ((2 * freqs + strip_rows, margin), bf16)],
        level_init, rows_mine, rows_other, tables["fwd"],
    )
    cols_mine = along("tx", send)
    cols_other = across(cols_mine)
    resist, grad = call(
        functools.partial(corner_kernel, counts),
        [((tile, tile), f32), ((2 * freqs, freqs), f32)],
        corner_doses, lift, cols_mine, cols_other, kernels, target,
        tables["fwd_t"], tables["inv"], tables["inv_t"],
        smem=1,
        scratch=[
            pltpu.VMEM((2 * freqs, count * freqs), bf16),
            pltpu.VMEM((2 * tile, count * freqs), bf16),
            pltpu.VMEM((count, tile, 2 * tile), f32),
            pltpu.VMEM((2 * tile, count * freqs), bf16),
        ],
    )
    grad = (grad + across(grad)).astype(bf16)
    grad_mine = along("tx", grad)
    grad_other = across(grad_mine)
    grad_lift, piece = call(
        functools.partial(lift_grad_kernel, counts),
        [((2 * freqs, tile + margin), bf16), ((margin + RIM, tile + margin), bf16)],
        grad, grad_mine, grad_other, tables["fwd"], tables["rim_cols"], tables["send_rows"],
    )
    piece_mine = along("ty", piece)
    piece_other = across(piece_mine)
    framed = (tile + RIM, tile + margin)
    own, frame, slope = call(
        functools.partial(frame_kernel, counts),
        [(framed, f32)] * 3,
        grad_lift, tables["own_rows"], level_init, rows_mine, rows_other, cols_mine, cols_other,
    )
    (level,) = call(
        functools.partial(advance_kernel, counts),
        [((tile, tile), f32)],
        own, piece_mine, piece_other, frame, slope,
        scratch=[pltpu.VMEM(framed, f32)]
        + [pltpu.VMEM((framed[0] + 2 * PAD, margin), f32)] * (2 * framed[1] // margin),
    )
    return (resist[None], level)


def solution(mesh):
    in_specs = (P("ty", "tx"), P("ty", "tx"), P("corner", None, None, None, None), P("corner"))
    out_specs = (P("corner", "ty", "tx"), P("ty", "tx"))
    return jax.shard_map(step, mesh=mesh, in_specs=in_specs, out_specs=out_specs, check_vma=False)
```

```python
import functools
import math

import jax
import jax.numpy as jnp
import numpy as np
from jax import lax
from jax.experimental import pallas as pl
from jax.experimental.pallas import tpu as pltpu
from jax.sharding import PartitionSpec as P

HALO = 128
KF = 128
LS_STEPS = 3

STEEPNESS = 4.0
THRESHOLD = 1.0
SPEED_GAIN = 4.0
SMOOTHING = 0.24
GRAD_FLOOR = 0.25

RIM = 16
PAD = 8
CHUNKS = 4
BLOCKS = 1
EDGE_PARTS = 4


def make_tables(tile, margin, freqs):
    window = tile + 2 * margin
    shifts = np.arange(freqs) - freqs // 2
    places = np.arange(window)
    angles = 2.0 * math.pi / window * (shifts[:, None] * places[None, :] % window)
    scaled = 1.0 / math.sqrt(window)
    cos = np.cos(angles) * scaled
    sin = np.sin(angles) * scaled
    stacked = np.concatenate([cos, -sin], axis=0)
    inv_cos = cos[:, margin : margin + tile].T
    inv_sin = sin[:, margin : margin + tile].T
    inverse = np.block([[inv_cos, -inv_sin], [inv_sin, inv_cos]])

    def rim(width, offset):
        out = np.zeros((2 * freqs, width))
        for step in range(LS_STEPS):
            for place, at in ((tile + step, step), (step - LS_STEPS, width - LS_STEPS + step)):
                if 0 <= place + offset < window:
                    out[:, at] = stacked[:, place + offset]
        return out

    offsets = (margin + tile, margin, margin - tile)
    rim_cols = np.stack([rim(margin, offset) for offset in offsets])
    rim_rows = [rim(RIM, offset).T for offset in offsets]
    own_rows = np.concatenate([stacked[:, margin : margin + tile].T, rim_rows[1]])
    send_rows = np.stack(
        [
            np.concatenate([stacked[:, :margin].T, rim_rows[2]]),
            np.concatenate([stacked[:, tile + margin :].T, rim_rows[0]]),
        ]
    )
    as_const = lambda values: np.asarray(values, np.float32).astype(jnp.bfloat16)
    return {
        "fwd": as_const(stacked),
        "fwd_t": as_const(stacked.T),
        "inv": as_const(inverse),
        "inv_t": as_const(inverse.T),
        "rim_cols": as_const(rim_cols),
        "own_rows": as_const(own_rows),
        "send_rows": as_const(send_rows),
    }


def dot(left, right):
    return jnp.dot(left, right, preferred_element_type=jnp.float32)


def dot_general(left, right, left_dim, right_dim):
    return lax.dot_general(
        left, right, (((left_dim,), (right_dim,)), ((), ())), preferred_element_type=jnp.float32
    )


def by_core(core, first, second):
    return jnp.where(core == 0, first, second)


def edge_kernel(level_ref, edge_ref, buffer_ref, sems):
    margin = edge_ref.shape[0]
    part = margin // EDGE_PARTS
    place = 1 - lax.rem(lax.axis_index("corner") + lax.axis_index("ty"), 2)
    copies = []
    for at in range(EDGE_PARTS):
        rows = pl.ds(pl.multiple_of(place * margin + at * part, part), part)
        copies.append(
            pltpu.make_async_copy(level_ref.at[rows, :], buffer_ref.at[at], sems.at[at])
        )
        copies[-1].start()
    for at, copy in enumerate(copies):
        copy.wait()
        values = buffer_ref[at].astype(jnp.float32) * 0.125
        edge_ref[at * part : (at + 1) * part] = values.astype(jnp.bfloat16)


def lift_kernel(counts, level_ref, mine_ref, other_ref, fwd_ref, lift_ref, send_ref):
    core = lax.axis_index("corner")
    tile = level_ref.shape[0]
    margin = mine_ref.shape[0]
    level = level_ref[...].astype(jnp.float32) * 0.125
    above, below = ordered("ty", counts, mine_ref[...], other_ref[...])
    above = above.astype(jnp.float32)
    below = below.astype(jnp.float32)
    squash = lambda values: jnp.tanh(0.25 * values).astype(jnp.bfloat16)
    lift = (
        dot(fwd_ref[:, :margin], squash(above))
        + dot(fwd_ref[:, margin : margin + tile], squash(level))
        + dot(fwd_ref[:, margin + tile :], squash(below))
    ).astype(jnp.bfloat16)
    lift_ref[...] = lift
    rows = lift.shape[0]
    send_ref[:rows, :] = by_core(core, lift[:, :margin], lift[:, tile - margin :])
    at = lax.broadcasted_iota(jnp.int32, (RIM, margin), 0)
    lane = lax.broadcasted_iota(jnp.int32, (RIM, margin), 1)
    first = by_core(core, 0, margin - LS_STEPS)
    pick = ((lane == first + at) & (at < LS_STEPS)).astype(jnp.bfloat16)
    rim = jnp.where(
        lax.broadcasted_iota(jnp.int32, (RIM, tile), 0) < RIM // 2,
        below[:RIM],
        above[margin - RIM :],
    )
    strip = by_core(core, level[:, :margin], level[:, tile - margin :]).astype(jnp.bfloat16)
    rim_strip = by_core(core, rim[:, :margin], rim[:, tile - margin :]).astype(jnp.bfloat16)
    for block in range(tile // margin):
        picked = dot_general(pick, strip[block * margin : (block + 1) * margin], 1, 1)
        send_ref[rows + block * RIM : rows + (block + 1) * RIM, :] = picked.astype(jnp.bfloat16)
    padded = jnp.concatenate([rim_strip, jnp.zeros((margin - RIM, margin), jnp.bfloat16)], axis=0)
    block = tile // margin
    send_ref[rows + block * RIM : rows + (block + 1) * RIM, :] = dot_general(
        pick, padded, 1, 1
    ).astype(jnp.bfloat16)


def corner_kernel(
    counts,
    dose_ref,
    lift_ref,
    mine_ref,
    other_ref,
    kernels_ref,
    target_ref,
    fwd_t_ref,
    inv_ref,
    inv_t_ref,
    resist_ref,
    grad_ref,
    blur_ref,
    proj_ref,
    field_ref,
    back_ref,
    done_ref,
    sems,
):
    tile = target_ref.shape[0]
    rows = lift_ref.shape[0]
    freqs = rows // 2
    margin = mine_ref.shape[1]
    count = kernels_ref.shape[0]
    left, right = ordered("tx", counts, mine_ref[:rows, :], other_ref[:rows, :])
    mixed = (
        dot(left, fwd_t_ref[:margin, :])
        + dot(lift_ref[...], fwd_t_ref[margin : margin + tile, :])
        + dot(right, fwd_t_ref[margin + tile :, :])
    )
    spec_re = mixed[:freqs, :freqs] - mixed[freqs:, freqs:]
    spec_im = mixed[:freqs, freqs:] + mixed[freqs:, :freqs]
    lanes = [slice(g * freqs, (g + 1) * freqs) for g in range(count)]
    groups = [range(g, min(g + 2, count)) for g in range(0, count, 2)]
    dose = dose_ref[0]
    size = tile // BLOCKS
    copies = []

    def project(group):
        for g in group:
            kernel_re = kernels_ref[g, 0]
            kernel_im = kernels_ref[g, 1]
            blur_re = (kernel_re * spec_re - kernel_im * spec_im).astype(jnp.bfloat16)
            blur_im = (kernel_re * spec_im + kernel_im * spec_re).astype(jnp.bfloat16)
            blur_ref[:freqs, lanes[g]] = blur_re
            blur_ref[freqs:, lanes[g]] = blur_im
        cols = slice(group[0] * freqs, (group[-1] + 1) * freqs)
        proj = dot(inv_ref[...], blur_ref[:, cols]).astype(jnp.bfloat16)
        for at, g in enumerate(group):
            for part in range(2):
                lane = (2 * g + part) * freqs
                proj_ref[:, lane : lane + freqs] = proj[part * tile : (part + 1) * tile, lanes[at]]

    def forward(block, g):
        at = slice(block * size, (block + 1) * size)
        pair = proj_ref[at, 2 * g * freqs : 2 * (g + 1) * freqs]
        field_ref[g, at] = dot(pair, inv_t_ref[...])

    def sensitivity(block):
        at = slice(block * size, (block + 1) * size)
        power = None
        for g in range(count):
            field = field_ref[g, at]
            term = field[:, :tile] * field[:, :tile] + field[:, tile:] * field[:, tile:]
            power = term if power is None else power + term
        resist = jax.nn.sigmoid(STEEPNESS * (dose * power - THRESHOLD))
        done_ref[at] = resist
        copies.append(
            pltpu.make_async_copy(done_ref.at[at, :], resist_ref.at[at, :], sems.at[block])
        )
        copies[-1].start()
        goal = target_ref[at].astype(jnp.float32)
        return (4.0 * STEEPNESS * dose) * (resist - goal) * (resist * (1.0 - resist))

    def backward(block, g, twice):
        at = slice(block * size, (block + 1) * size)
        adj_re = (twice * field_ref[g, at, :tile]).astype(jnp.bfloat16)
        adj_im = (twice * field_ref[g, at, tile:]).astype(jnp.bfloat16)
        adj = jnp.concatenate([adj_re, adj_im], axis=1)
        back = dot(adj, inv_ref[...]).astype(jnp.bfloat16)
        back_ref[block * size : (block + 1) * size, lanes[g]] = back[:, :freqs]
        back_ref[tile + block * size : tile + (block + 1) * size, lanes[g]] = back[:, freqs:]

    for group in groups:
        project(group)
    for g in range(count):
        forward(0, g)
    for block in range(BLOCKS):
        twice = sensitivity(block)
        for g in range(count):
            if block + 1 < BLOCKS:
                forward(block + 1, g)
        for g in range(count):
            backward(block, g, twice)
    grad_re = None
    for group in groups:
        cols = slice(group[0] * freqs, (group[-1] + 1) * freqs)
        blurred = dot(inv_t_ref[...], back_ref[:, cols])
        for at, g in enumerate(group):
            kernel_re = kernels_ref[g, 0]
            kernel_im = kernels_ref[g, 1]
            blur_re = blurred[:freqs, lanes[at]]
            blur_im = blurred[freqs:, lanes[at]]
            term_re = kernel_re * blur_re + kernel_im * blur_im
            term_im = kernel_re * blur_im - kernel_im * blur_re
            grad_re = term_re if grad_re is None else grad_re + term_re
            grad_im = term_im if g == 0 else grad_im + term_im
    grad_ref[:freqs, :] = grad_re
    grad_ref[freqs:, :] = grad_im
    for copy in copies:
        copy.wait()


def lift_grad_kernel(
    counts,
    grad_ref, mine_ref, other_ref, fwd_ref, rim_ref, send_rows_ref, lift_ref, send_ref
):
    to_after = 1 - lax.rem(lax.axis_index("corner") + lax.axis_index("ty"), 2)
    freqs = grad_ref.shape[0] // 2
    margin = rim_ref.shape[2]
    tile = fwd_ref.shape[1] - 2 * margin
    last = tile + margin

    def both(values):
        low_re = values[:freqs]
        low_im = values[freqs:]
        upper = jnp.concatenate([low_re, low_im], axis=1)
        lower = jnp.concatenate([low_im, -low_re], axis=1)
        return jnp.concatenate([upper, lower], axis=0)

    before, after = ordered("tx", counts, mine_ref[...], other_ref[...])
    before = both(before)
    here = both(grad_ref[...])
    after = both(after)
    middle = dot(here, fwd_ref[:, margin : margin + tile])
    lift_ref[:, :margin] = (middle[:, :margin] + dot(before, fwd_ref[:, last:])).astype(
        jnp.bfloat16
    )
    lift_ref[:, tile - margin : tile] = (
        middle[:, tile - margin :] + dot(after, fwd_ref[:, :margin])
    ).astype(jnp.bfloat16)
    lift_ref[:, tile:] = (
        dot(before, rim_ref[0]) + dot(here, rim_ref[1]) + dot(after, rim_ref[2])
    ).astype(jnp.bfloat16)
    send_ref[...] = dot(send_rows_ref[to_after], lift_ref[...]).astype(jnp.bfloat16)


def grid_masks(counts, margin):
    lane = lax.broadcasted_iota(jnp.int32, (PAD, margin), 1)
    at_ty, at_tx = lax.axis_index("ty"), lax.axis_index("tx")
    every = lane >= 0
    above = every & (at_ty > 0)
    below = every & (at_ty < counts["ty"] - 1)
    beside = ((lane >= margin // 2) & (at_tx > 0)) | (
        (lane < margin // 2) & (at_tx < counts["tx"] - 1)
    )
    return above, below, beside


def within(keeps, rows, blocks, at, block, level):
    above, below, beside = keeps
    if at == 0:
        level = jnp.where(above, level, 0.0)
    if at == rows - PAD:
        level = jnp.where(below, level, 0.0)
    if block == blocks - 1:
        level = jnp.where(beside, level, 0.0)
    return level


def stencil(source, at, wanted, margin):
    blocks = len(source)
    lane = lax.broadcasted_iota(jnp.int32, (PAD, margin), 1)
    here = [ref[PAD + at : 2 * PAD + at] for ref in source]
    back = [pltpu.roll(part, 1, 1) for part in here]
    ahead = [pltpu.roll(part, margin - 1, 1) for part in here]
    for block in range(wanted):
        up = source[block][PAD + at - 1 : 2 * PAD + at - 1]
        down = source[block][PAD + at + 1 : 2 * PAD + at + 1]
        left = jnp.where(lane == 0, back[block - 1], back[block])
        right = jnp.where(lane == margin - 1, ahead[(block + 1) % blocks], ahead[block])
        slope_y = down - up
        slope_x = right - left
        square = GRAD_FLOOR + slope_y * slope_y + slope_x * slope_x
        base = (1.0 - 4.0 * SMOOTHING) * here[block] + SMOOTHING * ((up + down) + (left + right))
        yield base, square * lax.rsqrt(square)


def frame_kernel(
    counts,
    lift_ref, own_rows_ref, level_ref, mine_ref, other_ref, cols_mine_ref, cols_other_ref,
    grad_ref, slope_ref, base_ref, root_ref, *level_refs,
):
    tile = level_ref.shape[0]
    margin = mine_ref.shape[0]
    rows = lift_ref.shape[0]
    grad_ref[...] = dot(own_rows_ref[...], lift_ref[...])
    above, below = ordered("ty", counts, mine_ref[...], other_ref[...])
    blocks = len(level_refs)
    extent = slope_ref.shape[0]
    level = level_ref[...].astype(jnp.float32) * 0.0625
    above = 0.5 * above.astype(jnp.float32)[margin - PAD :]
    below = 0.5 * below.astype(jnp.float32)[:PAD]
    zero = jnp.zeros((PAD, margin), jnp.float32)
    for block, ref in enumerate(level_refs):
        ref[:PAD] = zero
        ref[PAD + extent :] = zero
        if block < blocks - 1:
            lanes = slice(block * margin, (block + 1) * margin)
            ref[PAD : 2 * PAD] = above[:, lanes]
            ref[2 * PAD : 2 * PAD + tile] = level[:, lanes]
            ref[2 * PAD + tile : PAD + extent] = below[:, lanes]
    at = lax.broadcasted_iota(jnp.int32, (RIM, margin), 0)
    lane = lax.broadcasted_iota(jnp.int32, (RIM, margin), 1)
    place_left = ((lane == margin - LS_STEPS + at) & (at < LS_STEPS)).astype(jnp.bfloat16)
    place_right = ((lane == at) & (at < LS_STEPS)).astype(jnp.bfloat16)
    side = level_refs[-1]
    for block in range(tile // margin + 1):
        part = slice(rows + block * RIM, rows + (block + 1) * RIM)
        left, right = ordered("tx", counts, cols_mine_ref[part, :], cols_other_ref[part, :])
        placed = dot_general(left, place_left, 0, 0) + dot_general(right, place_right, 0, 0)
        placed = 0.5 * placed
        if block < tile // margin:
            start = 2 * PAD + block * margin
            side[start : start + margin] = placed
        else:
            side[2 * PAD + tile : PAD + extent] = placed[:PAD]
            side[PAD : 2 * PAD] = placed[PAD:RIM]
    for at in range(0, extent, PAD):
        for block, (base, root) in enumerate(stencil(level_refs, at, blocks, margin)):
            lanes = slice(block * margin, (block + 1) * margin)
            trans = jnp.tanh(0.5 * level_refs[block][PAD + at : 2 * PAD + at])
            base_ref[at : at + PAD, lanes] = base
            root_ref[at : at + PAD, lanes] = root
            slope_ref[at : at + PAD, lanes] = (SPEED_GAIN * 0.5 * 0.25) * (1.0 - trans * trans)


def advance_kernel(
    counts, grad_ref, mine_ref, other_ref, slope_ref, base_ref, root_ref, out_ref,
    speed_ref, done_ref, sems, *level_refs,
):
    rows, cols = slope_ref.shape
    tile = out_ref.shape[0]
    margin = cols - tile
    blocks = cols // margin
    first, last = level_refs[:blocks], level_refs[blocks:]
    keeps = grid_masks(counts, margin)
    before, after = ordered("ty", counts, mine_ref[...], other_ref[...])
    before = before.astype(jnp.float32)
    after = after.astype(jnp.float32)
    rim = before[margin:] + after[margin:] + grad_ref[tile:]
    speed_ref[:PAD] = rim[PAD:] * slope_ref[:PAD]
    speed_ref[PAD + tile :] = rim[:PAD] * slope_ref[PAD + tile :]
    for half, part in ((0, before), (1, after)):
        at = half * margin
        speed_ref[PAD + at : PAD + at + margin] = (
            grad_ref[at : at + margin] + part[:margin]
        ) * slope_ref[PAD + at : PAD + at + margin]
    for ref in level_refs:
        ref[:PAD] = jnp.zeros((PAD, margin), jnp.float32)
        ref[PAD + rows :] = jnp.zeros((PAD, margin), jnp.float32)

    def store(target, at, block, level):
        level = within(keeps, rows, blocks, at, block, level)
        target[block][PAD + at : 2 * PAD + at] = level

    for at in range(0, rows, PAD):
        for block in range(blocks):
            lanes = slice(block * margin, (block + 1) * margin)
            level = (
                base_ref[at : at + PAD, lanes]
                - speed_ref[at : at + PAD, lanes] * root_ref[at : at + PAD, lanes]
            )
            store(first, at, block, level)
    source, target = first, last
    copies = []
    for step in range(1, LS_STEPS):
        final = step == LS_STEPS - 1
        for at in range(PAD if final else 0, rows - PAD if final else rows, PAD):
            parts = list(stencil(source, at, blocks - 1 if final else blocks, margin))
            for block, (base, root) in enumerate(parts):
                lanes = slice(block * margin, (block + 1) * margin)
                level = base - speed_ref[at : at + PAD, lanes] * root
                if final:
                    done_ref[at - PAD : at, lanes] = 2.0 * level
                else:
                    store(target, at, block, level)
            chunk = tile // CHUNKS
            if final and at % chunk == 0:
                piece = slice(at - chunk, at)
                copy = pltpu.make_async_copy(
                    done_ref.at[piece, :], out_ref.at[piece, :], sems.at[at // chunk - 1]
                )
                copy.start()
                copies.append(copy)
        source, target = target, source
    for copy in copies:
        copy.wait()


def load_kernel(*refs):
    count = len(refs) // 2
    sems = refs[-1]
    copies = [
        pltpu.make_async_copy(refs[i], refs[count + i], sems.at[i]) for i in range(count)
    ]
    for copy in copies:
        copy.start()
    for copy in copies:
        copy.wait()


def load(*arrays):
    return pl.pallas_call(
        load_kernel,
        out_shape=[jax.ShapeDtypeStruct(item.shape, item.dtype) for item in arrays],
        in_specs=[pl.BlockSpec(memory_space=pltpu.HBM)] * len(arrays),
        out_specs=[pl.BlockSpec(memory_space=pltpu.VMEM)] * len(arrays),
        scratch_shapes=[pltpu.SemaphoreType.DMA((len(arrays),))],
        compiler_params=pltpu.CompilerParams(vmem_limit_bytes=24 << 20),
        cost_estimate=pl.CostEstimate(flops=0, bytes_accessed=8 << 20, transcendentals=0),
        name="load",
    )(*[pltpu.with_memory_space_constraint(item, pltpu.HBM) for item in arrays])


def call(kernel, out_shape, *args, scratch=(), smem=0, out_space=()):
    vmem = pl.BlockSpec(memory_space=pltpu.VMEM)
    in_specs = [pl.BlockSpec(memory_space=pltpu.SMEM)] * smem + [vmem] * (len(args) - smem)
    return pl.pallas_call(
        kernel,
        out_shape=[jax.ShapeDtypeStruct(*item) for item in out_shape],
        in_specs=in_specs,
        out_specs=[pl.BlockSpec(memory_space=space) for space in out_space or [pltpu.VMEM] * len(out_shape)],
        scratch_shapes=list(scratch),
        compiler_params=pltpu.CompilerParams(vmem_limit_bytes=24 << 20),
    )(*args)


def along(axis, values):
    rows, cols = lax.axis_size("ty"), lax.axis_size("tx")
    count, others = (rows, cols) if axis == "ty" else (cols, rows)

    def device(place, other, core):
        row, col = (place, other) if axis == "ty" else (other, place)
        return (row * cols + col) * 2 + core

    pairs = []
    for other in range(others):
        free = {device(place, other, core) for place in (0, count - 1) for core in range(2)}
        for place in range(count - 1):
            cores = (place % 2, place % 2) if axis == "ty" else (1, 0)
            one, two = device(place, other, cores[0]), device(place + 1, other, cores[1])
            pairs += [(one, two), (two, one)]
            free -= {one, two}
        if other % 2 == 0 and other + 1 < others:
            step = device(0, 1, 0) - device(0, 0, 0)
            for one in sorted(free):
                pairs += [(one, one + step), (one + step, one)]
    return lax.ppermute(values, ("ty", "tx", "corner"), pairs)


def ordered(axis, counts, mine, other):
    index, core = lax.axis_index(axis), lax.axis_index("corner")
    count = counts[axis]
    from_before = (core != lax.rem(index, 2)) if axis == "ty" else core == 0
    before = jnp.where(from_before, mine, other)
    after = jnp.where(from_before, other, mine)
    zero = jnp.zeros_like(mine)
    return jnp.where(index > 0, before, zero), jnp.where(index < count - 1, after, zero)


def across(values):
    return lax.ppermute(values, "corner", [(0, 1), (1, 0)])


def step(level_init, target, kernels, corner_doses):
    tile = level_init.shape[0]
    margin = HALO
    freqs = KF
    count = kernels.shape[1]
    tables = make_tables(tile, margin, freqs)
    bf16, f32 = jnp.bfloat16, jnp.float32
    counts = {"ty": lax.axis_size("ty"), "tx": lax.axis_size("tx")}
    edge = pl.pallas_call(
        edge_kernel,
        out_shape=jax.ShapeDtypeStruct((margin, tile), bf16),
        in_specs=[pl.BlockSpec(memory_space=pltpu.HBM)],
        out_specs=pl.BlockSpec(memory_space=pltpu.VMEM),
        scratch_shapes=[
            pltpu.VMEM((EDGE_PARTS, margin // EDGE_PARTS, tile), level_init.dtype),
            pltpu.SemaphoreType.DMA((EDGE_PARTS,)),
        ],
        compiler_params=pltpu.CompilerParams(vmem_limit_bytes=24 << 20),
        name="edge",
    )(pltpu.with_memory_space_constraint(level_init, pltpu.HBM))
    rows_mine = along("ty", edge)
    rows_other = across(rows_mine)
    names = sorted(tables)
    level_init, target, kernels, *loaded = load(
        level_init, target, kernels[0], *(tables[name] for name in names)
    )
    tables = dict(zip(names, loaded))
    strip_rows = (tile // margin + 1) * RIM
    lift, send = call(
        functools.partial(lift_kernel, counts),
        [((2 * freqs, tile), bf16), ((2 * freqs + strip_rows, margin), bf16)],
        level_init, rows_mine, rows_other, tables["fwd"],
    )
    cols_mine = along("tx", send)
    cols_other = across(cols_mine)
    resist, grad = call(
        functools.partial(corner_kernel, counts),
        [((tile, tile), f32), ((2 * freqs, freqs), f32)],
        corner_doses, lift, cols_mine, cols_other, kernels, target,
        tables["fwd_t"], tables["inv"], tables["inv_t"],
        smem=1,
        scratch=[
            pltpu.VMEM((2 * freqs, count * freqs), bf16),
            pltpu.VMEM((tile, 2 * count * freqs), bf16),
            pltpu.VMEM((count, tile, 2 * tile), f32),
            pltpu.VMEM((2 * tile, count * freqs), bf16),
            pltpu.VMEM((tile, tile), f32),
            pltpu.SemaphoreType.DMA((BLOCKS,)),
        ],
        out_space=(pltpu.HBM, pltpu.VMEM),
    )
    grad = (grad + across(grad)).astype(bf16)
    grad_mine = along("tx", grad)
    grad_other = across(grad_mine)
    grad_lift, piece = call(
        functools.partial(lift_grad_kernel, counts),
        [((2 * freqs, tile + margin), bf16), ((margin + RIM, tile + margin), bf16)],
        grad, grad_mine, grad_other, tables["fwd"], tables["rim_cols"], tables["send_rows"],
    )
    piece_mine = along("ty", piece)
    piece_other = across(piece_mine)
    framed = (tile + RIM, tile + margin)
    levels = [pltpu.VMEM((framed[0] + 2 * PAD, margin), f32)] * (framed[1] // margin)
    frame = call(
        functools.partial(frame_kernel, counts),
        [(framed, f32)] * 4,
        grad_lift, tables["own_rows"], level_init, rows_mine, rows_other, cols_mine, cols_other,
        scratch=levels,
    )
    (level,) = call(
        functools.partial(advance_kernel, counts),
        [((tile, tile), f32)],
        frame[0], piece_mine, piece_other, *frame[1:],
        out_space=(pltpu.HBM,),
        scratch=[
            pltpu.VMEM(framed, f32),
            pltpu.VMEM((tile, tile), f32),
            pltpu.SemaphoreType.DMA((CHUNKS,)),
        ]
        + levels * 2,
    )
    return (resist[None], level)


def solution(mesh):
    in_specs = (P("ty", "tx"), P("ty", "tx"), P("corner", None, None, None, None), P("corner"))
    out_specs = (P("corner", "ty", "tx"), P("ty", "tx"))
    return jax.shard_map(step, mesh=mesh, in_specs=in_specs, out_specs=out_specs, check_vma=False)
```

```python
import functools
import math

import jax
import jax.numpy as jnp
import numpy as np
from jax import lax
from jax.experimental import pallas as pl
from jax.experimental.pallas import tpu as pltpu
from jax.sharding import PartitionSpec as P

HALO = 128
KF = 128
LS_STEPS = 3

STEEPNESS = 4.0
THRESHOLD = 1.0
SPEED_GAIN = 4.0
SMOOTHING = 0.24
GRAD_FLOOR = 0.25

RIM = 16
PAD = 8
CHUNKS = 4
BLOCKS = 1
EDGE_PARTS = 4


def make_tables(tile, margin, freqs):
    window = tile + 2 * margin
    shifts = np.arange(freqs) - freqs // 2
    places = np.arange(window)
    angles = 2.0 * math.pi / window * (shifts[:, None] * places[None, :] % window)
    scaled = 1.0 / math.sqrt(window)
    cos = np.cos(angles) * scaled
    sin = np.sin(angles) * scaled
    stacked = np.concatenate([cos, -sin], axis=0)
    inv_cos = cos[:, margin : margin + tile].T
    inv_sin = sin[:, margin : margin + tile].T
    inverse = np.block([[inv_cos, -inv_sin], [inv_sin, inv_cos]])

    def rim(width, offset):
        out = np.zeros((2 * freqs, width))
        for step in range(LS_STEPS):
            for place, at in ((tile + step, step), (step - LS_STEPS, width - LS_STEPS + step)):
                if 0 <= place + offset < window:
                    out[:, at] = stacked[:, place + offset]
        return out

    offsets = (margin + tile, margin, margin - tile)
    rim_cols = np.stack([rim(margin, offset) for offset in offsets])
    rim_rows = [rim(RIM, offset).T for offset in offsets]
    own_rows = np.concatenate([stacked[:, margin : margin + tile].T, rim_rows[1]])
    send_rows = np.stack(
        [
            np.concatenate([stacked[:, :margin].T, rim_rows[2][:PAD]]),
            np.concatenate([stacked[:, tile + margin :].T, rim_rows[0][PAD:]]),
        ]
    )
    half = freqs // 2
    packed = np.concatenate([stacked[:half], stacked[freqs : freqs + half], np.zeros((RIM, window))])
    packed[2 * half] = stacked[half]
    expand = np.zeros((2 * freqs, 2 * half + RIM))
    for row in range(freqs):
        mirror = row if row <= half else freqs - row
        expand[row, mirror if row != half else 2 * half] = 1.0
        if row != half:
            expand[freqs + row, half + mirror] = 1.0 if row < half else -1.0
    middle = slice(margin, margin + tile)
    by_place = np.concatenate([stacked[:, middle], stacked[:, :margin], stacked[:, tile + margin :]], 1).T
    as_const = lambda values: np.asarray(values, np.float32).astype(jnp.bfloat16)
    return {
        "fwd": as_const(stacked),
        "fwd_t": as_const(by_place),
        "packed": as_const(packed),
        "expand": as_const(expand),
        "inv": as_const(inverse),
        "inv_t": as_const(inverse.T),
        "rim_cols": as_const(rim_cols),
        "own_rows": as_const(own_rows),
        "send_rows": as_const(send_rows),
    }


def dot(left, right):
    return jnp.dot(left, right, preferred_element_type=jnp.float32)


def dot_general(left, right, left_dim, right_dim):
    return lax.dot_general(
        left, right, (((left_dim,), (right_dim,)), ((), ())), preferred_element_type=jnp.float32
    )


def by_core(core, first, second):
    return jnp.where(core == 0, first, second)


def edge_kernel(level_ref, edge_ref, buffer_ref, sems):
    margin = edge_ref.shape[0]
    part = margin // EDGE_PARTS
    place = 1 - lax.rem(lax.axis_index("corner") + lax.axis_index("ty"), 2)
    copies = []
    for at in range(EDGE_PARTS):
        rows = pl.ds(pl.multiple_of(place * margin + at * part, part), part)
        copies.append(
            pltpu.make_async_copy(level_ref.at[rows, :], buffer_ref.at[at], sems.at[at])
        )
        copies[-1].start()
    for at, copy in enumerate(copies):
        copy.wait()
        values = buffer_ref[at].astype(jnp.float32) * 0.125
        edge_ref[at * part : (at + 1) * part] = values.astype(jnp.bfloat16)


def squash(values):
    return jnp.tanh(0.25 * values).astype(jnp.bfloat16)


def rim_picker(margin):
    at = lax.broadcasted_iota(jnp.int32, (RIM, margin), 0)
    lane = lax.broadcasted_iota(jnp.int32, (RIM, margin), 1)
    first = by_core(lax.axis_index("corner"), 0, margin - LS_STEPS)
    return ((lane == first + at) & (at < LS_STEPS)).astype(jnp.bfloat16)


def own_lift_kernel(level_ref, packed_ref, lift_ref, strip_ref):
    core = lax.axis_index("corner")
    tile = level_ref.shape[0]
    margin = strip_ref.shape[1]
    level = level_ref[...].astype(jnp.float32) * 0.125
    lift_ref[...] = dot(packed_ref[:, margin : margin + tile], squash(level))
    strip = by_core(core, level[:, :margin], level[:, tile - margin :]).astype(jnp.bfloat16)
    pick = rim_picker(margin)
    for block in range(tile // margin):
        rows = strip[block * margin : (block + 1) * margin]
        picked = dot_general(pick, rows, 1, 1).astype(jnp.bfloat16)
        strip_ref[block * RIM : (block + 1) * RIM] = picked


def lift_kernel(counts, lift_ref, strip_ref, mine_ref, other_ref, packed_ref, send_ref):
    core = lax.axis_index("corner")
    margin, tile = mine_ref.shape
    rows = lift_ref.shape[0]
    lanes = pl.ds(pl.multiple_of(core * (tile - margin), margin), margin)
    above, below = ordered("ty", counts, mine_ref[:, lanes], other_ref[:, lanes])
    above = above.astype(jnp.float32)
    below = below.astype(jnp.float32)
    send_ref[:rows, :] = (
        lift_ref[:, lanes]
        + dot(packed_ref[:, :margin], squash(above))
        + dot(packed_ref[:, margin + tile :], squash(below))
    ).astype(jnp.bfloat16)
    strips = strip_ref.shape[0]
    send_ref[rows : rows + strips, :] = strip_ref[...]
    rim = jnp.where(
        lax.broadcasted_iota(jnp.int32, (RIM, margin), 0) < PAD, below[:RIM], above[margin - RIM :]
    )
    rim = jnp.concatenate([rim, jnp.zeros((margin - RIM, margin), jnp.float32)], axis=0)
    picked = dot_general(rim_picker(margin), rim.astype(jnp.bfloat16), 1, 1)
    send_ref[rows + strips :, :] = picked.astype(jnp.bfloat16)


def own_spec_kernel(
    counts, lift_ref, mine_ref, other_ref, packed_ref, expand_ref, fwd_t_ref, mixed_ref
):
    margin, tile = mine_ref.shape
    above, below = ordered("ty", counts, mine_ref[...], other_ref[...])
    lift = (
        lift_ref[...]
        + dot(packed_ref[:, :margin], squash(above.astype(jnp.float32)))
        + dot(packed_ref[:, margin + tile :], squash(below.astype(jnp.float32)))
    ).astype(jnp.bfloat16)
    lift = dot(expand_ref[...], lift).astype(jnp.bfloat16)
    mixed_ref[...] = dot(lift, fwd_t_ref[:tile])


def corner_kernel(
    counts,
    dose_ref,
    mixed_ref,
    mine_ref,
    other_ref,
    kernels_ref,
    target_ref,
    expand_ref,
    fwd_t_ref,
    inv_ref,
    inv_t_ref,
    resist_ref,
    grad_ref,
    blur_ref,
    proj_ref,
    field_ref,
    back_ref,
    done_ref,
    sems,
):
    tile = target_ref.shape[0]
    freqs = expand_ref.shape[0] // 2
    rows = expand_ref.shape[1]
    count = kernels_ref.shape[0]
    sides = ordered("tx", counts, mine_ref[:rows, :], other_ref[:rows, :])
    sides = dot(expand_ref[...], jnp.concatenate(sides, axis=1)).astype(jnp.bfloat16)
    mixed = mixed_ref[...] + dot(sides, fwd_t_ref[tile:])
    spec_re = mixed[:freqs, :freqs] - mixed[freqs:, freqs:]
    spec_im = mixed[:freqs, freqs:] + mixed[freqs:, :freqs]
    lanes = [slice(g * freqs, (g + 1) * freqs) for g in range(count)]
    groups = [range(g, min(g + 2, count)) for g in range(0, count, 2)]
    dose = dose_ref[0]
    size = tile // BLOCKS
    copies = []

    def project(group):
        for g in group:
            kernel_re = kernels_ref[g, 0]
            kernel_im = kernels_ref[g, 1]
            blur_re = (kernel_re * spec_re - kernel_im * spec_im).astype(jnp.bfloat16)
            blur_im = (kernel_re * spec_im + kernel_im * spec_re).astype(jnp.bfloat16)
            blur_ref[:freqs, lanes[g]] = blur_re
            blur_ref[freqs:, lanes[g]] = blur_im
        cols = slice(group[0] * freqs, (group[-1] + 1) * freqs)
        proj = dot(inv_ref[...], blur_ref[:, cols]).astype(jnp.bfloat16)
        for at, g in enumerate(group):
            for part in range(2):
                lane = (2 * g + part) * freqs
                proj_ref[:, lane : lane + freqs] = proj[part * tile : (part + 1) * tile, lanes[at]]

    def forward(block, g):
        at = slice(block * size, (block + 1) * size)
        pair = proj_ref[at, 2 * g * freqs : 2 * (g + 1) * freqs]
        field_ref[g, at] = dot(pair, inv_t_ref[...])

    def sensitivity(block):
        at = slice(block * size, (block + 1) * size)
        power = None
        for g in range(count):
            field = field_ref[g, at]
            term = field[:, :tile] * field[:, :tile] + field[:, tile:] * field[:, tile:]
            power = term if power is None else power + term
        resist = jax.nn.sigmoid(STEEPNESS * (dose * power - THRESHOLD))
        done_ref[at] = resist
        copies.append(
            pltpu.make_async_copy(done_ref.at[at, :], resist_ref.at[at, :], sems.at[block])
        )
        copies[-1].start()
        goal = target_ref[at].astype(jnp.float32)
        return (4.0 * STEEPNESS * dose) * (resist - goal) * (resist * (1.0 - resist))

    def backward(block, g, twice):
        at = slice(block * size, (block + 1) * size)
        adj_re = (twice * field_ref[g, at, :tile]).astype(jnp.bfloat16)
        adj_im = (twice * field_ref[g, at, tile:]).astype(jnp.bfloat16)
        adj = jnp.concatenate([adj_re, adj_im], axis=1)
        back = dot(adj, inv_ref[...]).astype(jnp.bfloat16)
        back_ref[block * size : (block + 1) * size, lanes[g]] = back[:, :freqs]
        back_ref[tile + block * size : tile + (block + 1) * size, lanes[g]] = back[:, freqs:]

    for group in groups:
        project(group)
    for g in range(count):
        forward(0, g)
    for block in range(BLOCKS):
        twice = sensitivity(block)
        for g in range(count):
            if block + 1 < BLOCKS:
                forward(block + 1, g)
        for g in range(count):
            backward(block, g, twice)
    grad_re = None
    for group in groups:
        cols = slice(group[0] * freqs, (group[-1] + 1) * freqs)
        blurred = dot(inv_t_ref[...], back_ref[:, cols])
        for at, g in enumerate(group):
            kernel_re = kernels_ref[g, 0]
            kernel_im = kernels_ref[g, 1]
            blur_re = blurred[:freqs, lanes[at]]
            blur_im = blurred[freqs:, lanes[at]]
            term_re = kernel_re * blur_re + kernel_im * blur_im
            term_im = kernel_re * blur_im - kernel_im * blur_re
            grad_re = term_re if grad_re is None else grad_re + term_re
            grad_im = term_im if g == 0 else grad_im + term_im
    grad_ref[:freqs, :] = grad_re
    grad_ref[freqs:, :] = grad_im
    for copy in copies:
        copy.wait()


def both_parts(values):
    freqs = values.shape[0] // 2
    low_re = values[:freqs]
    low_im = values[freqs:]
    upper = jnp.concatenate([low_re, low_im], axis=1)
    lower = jnp.concatenate([low_im, -low_re], axis=1)
    return jnp.concatenate([upper, lower], axis=0)


def own_grad_kernel(grad_ref, fwd_ref, rim_ref, lift_ref):
    margin = rim_ref.shape[2]
    tile = fwd_ref.shape[1] - 2 * margin
    here = both_parts(grad_ref[...])
    lift_ref[:, :tile] = dot(here, fwd_ref[:, margin : margin + tile])
    lift_ref[:, tile:] = dot(here, rim_ref[1])


def lift_grad_kernel(
    counts, own_ref, mine_ref, other_ref, fwd_ref, rim_ref, send_rows_ref, lift_ref, send_ref
):
    to_after = 1 - lax.rem(lax.axis_index("corner") + lax.axis_index("ty"), 2)
    margin = rim_ref.shape[2]
    tile = fwd_ref.shape[1] - 2 * margin
    before, after = ordered("tx", counts, mine_ref[...], other_ref[...])
    before = both_parts(before)
    after = both_parts(after)
    first = own_ref[:, :margin] + dot(before, fwd_ref[:, tile + margin :])
    last = own_ref[:, tile - margin : tile] + dot(after, fwd_ref[:, :margin])
    rim = own_ref[:, tile:] + dot(before, rim_ref[0]) + dot(after, rim_ref[2])
    lift_ref[:, :margin] = first.astype(jnp.bfloat16)
    lift_ref[:, tile - margin : tile] = last.astype(jnp.bfloat16)
    lift_ref[:, tile:] = rim.astype(jnp.bfloat16)
    send_ref[...] = dot(send_rows_ref[to_after], lift_ref[...]).astype(jnp.bfloat16)


def grid_masks(counts, margin):
    lane = lax.broadcasted_iota(jnp.int32, (PAD, margin), 1)
    at_ty, at_tx = lax.axis_index("ty"), lax.axis_index("tx")
    every = lane >= 0
    above = every & (at_ty > 0)
    below = every & (at_ty < counts["ty"] - 1)
    beside = ((lane >= margin // 2) & (at_tx > 0)) | (
        (lane < margin // 2) & (at_tx < counts["tx"] - 1)
    )
    return above, below, beside


def within(keeps, rows, blocks, at, block, level):
    above, below, beside = keeps
    if at == 0:
        level = jnp.where(above, level, 0.0)
    if at == rows - PAD:
        level = jnp.where(below, level, 0.0)
    if block == blocks - 1:
        level = jnp.where(beside, level, 0.0)
    return level


def stencil(source, at, wanted, margin):
    blocks = len(source)
    lane = lax.broadcasted_iota(jnp.int32, (PAD, margin), 1)
    here = [ref[PAD + at : 2 * PAD + at] for ref in source]
    back = [pltpu.roll(part, 1, 1) for part in here]
    ahead = [pltpu.roll(part, margin - 1, 1) for part in here]
    for block in range(wanted):
        up = source[block][PAD + at - 1 : 2 * PAD + at - 1]
        down = source[block][PAD + at + 1 : 2 * PAD + at + 1]
        left = jnp.where(lane == 0, back[block - 1], back[block])
        right = jnp.where(lane == margin - 1, ahead[(block + 1) % blocks], ahead[block])
        slope_y = down - up
        slope_x = right - left
        square = GRAD_FLOOR + slope_y * slope_y + slope_x * slope_x
        base = (1.0 - 4.0 * SMOOTHING) * here[block] + SMOOTHING * ((up + down) + (left + right))
        yield base, square * lax.rsqrt(square)


def frame_kernel(
    counts,
    lift_ref, own_rows_ref, level_ref, mine_ref, other_ref, cols_mine_ref, cols_other_ref,
    grad_ref, slope_ref, base_ref, root_ref, *level_refs,
):
    tile = level_ref.shape[0]
    margin = mine_ref.shape[0]
    grad_ref[...] = dot(own_rows_ref[...], lift_ref[...])
    rows = cols_mine_ref.shape[0] - (tile // margin + 1) * RIM
    above, below = ordered("ty", counts, mine_ref[...], other_ref[...])
    blocks = len(level_refs)
    extent = slope_ref.shape[0]
    level = level_ref[...].astype(jnp.float32) * 0.0625
    above = 0.5 * above.astype(jnp.float32)[margin - PAD :]
    below = 0.5 * below.astype(jnp.float32)[:PAD]
    zero = jnp.zeros((PAD, margin), jnp.float32)
    for block, ref in enumerate(level_refs):
        ref[:PAD] = zero
        ref[PAD + extent :] = zero
        if block < blocks - 1:
            lanes = slice(block * margin, (block + 1) * margin)
            ref[PAD : 2 * PAD] = above[:, lanes]
            ref[2 * PAD : 2 * PAD + tile] = level[:, lanes]
            ref[2 * PAD + tile : PAD + extent] = below[:, lanes]
    at = lax.broadcasted_iota(jnp.int32, (RIM, margin), 0)
    lane = lax.broadcasted_iota(jnp.int32, (RIM, margin), 1)
    place_left = ((lane == margin - LS_STEPS + at) & (at < LS_STEPS)).astype(jnp.bfloat16)
    place_right = ((lane == at) & (at < LS_STEPS)).astype(jnp.bfloat16)
    side = level_refs[-1]
    for block in range(tile // margin + 1):
        part = slice(rows + block * RIM, rows + (block + 1) * RIM)
        left, right = ordered("tx", counts, cols_mine_ref[part, :], cols_other_ref[part, :])
        placed = dot_general(left, place_left, 0, 0) + dot_general(right, place_right, 0, 0)
        placed = 0.5 * placed
        if block < tile // margin:
            start = 2 * PAD + block * margin
            side[start : start + margin] = placed
        else:
            side[2 * PAD + tile : PAD + extent] = placed[:PAD]
            side[PAD : 2 * PAD] = placed[PAD:RIM]
    for at in range(0, extent, PAD):
        for block, (base, root) in enumerate(stencil(level_refs, at, blocks, margin)):
            lanes = slice(block * margin, (block + 1) * margin)
            trans = jnp.tanh(0.5 * level_refs[block][PAD + at : 2 * PAD + at])
            base_ref[at : at + PAD, lanes] = base
            root_ref[at : at + PAD, lanes] = root
            slope_ref[at : at + PAD, lanes] = (SPEED_GAIN * 0.5 * 0.25) * (1.0 - trans * trans)


def advance_kernel(
    counts, grad_ref, mine_ref, other_ref, slope_ref, base_ref, root_ref, out_ref,
    speed_ref, done_ref, sems, *level_refs,
):
    rows, cols = slope_ref.shape
    tile = out_ref.shape[0]
    margin = cols - tile
    blocks = cols // margin
    first, last = level_refs[:blocks], level_refs[blocks:]
    keeps = grid_masks(counts, margin)
    before, after = ordered("ty", counts, mine_ref[...], other_ref[...])
    before = before.astype(jnp.float32)
    after = after.astype(jnp.float32)
    speed_ref[:PAD] = (before[margin:] + grad_ref[tile + PAD :]) * slope_ref[:PAD]
    speed_ref[PAD + tile :] = (after[margin:] + grad_ref[tile : tile + PAD]) * slope_ref[PAD + tile :]
    for half, part in ((0, before), (1, after)):
        at = half * margin
        speed_ref[PAD + at : PAD + at + margin] = (
            grad_ref[at : at + margin] + part[:margin]
        ) * slope_ref[PAD + at : PAD + at + margin]
    for ref in level_refs:
        ref[:PAD] = jnp.zeros((PAD, margin), jnp.float32)
        ref[PAD + rows :] = jnp.zeros((PAD, margin), jnp.float32)

    def store(target, at, block, level):
        level = within(keeps, rows, blocks, at, block, level)
        target[block][PAD + at : 2 * PAD + at] = level

    for at in range(0, rows, PAD):
        for block in range(blocks):
            lanes = slice(block * margin, (block + 1) * margin)
            level = (
                base_ref[at : at + PAD, lanes]
                - speed_ref[at : at + PAD, lanes] * root_ref[at : at + PAD, lanes]
            )
            store(first, at, block, level)
    source, target = first, last
    copies = []
    for step in range(1, LS_STEPS):
        final = step == LS_STEPS - 1
        for at in range(PAD if final else 0, rows - PAD if final else rows, PAD):
            parts = list(stencil(source, at, blocks - 1 if final else blocks, margin))
            for block, (base, root) in enumerate(parts):
                lanes = slice(block * margin, (block + 1) * margin)
                level = base - speed_ref[at : at + PAD, lanes] * root
                if final:
                    done_ref[at - PAD : at, lanes] = 2.0 * level
                else:
                    store(target, at, block, level)
            chunk = tile // CHUNKS
            if final and at % chunk == 0:
                piece = slice(at - chunk, at)
                copy = pltpu.make_async_copy(
                    done_ref.at[piece, :], out_ref.at[piece, :], sems.at[at // chunk - 1]
                )
                copy.start()
                copies.append(copy)
        source, target = target, source
    for copy in copies:
        copy.wait()


def load_kernel(*refs):
    count = len(refs) // 2
    sems = refs[-1]
    copies = [
        pltpu.make_async_copy(refs[i], refs[count + i], sems.at[i]) for i in range(count)
    ]
    for copy in copies:
        copy.start()
    for copy in copies:
        copy.wait()


def load(*arrays):
    return pl.pallas_call(
        load_kernel,
        out_shape=[jax.ShapeDtypeStruct(item.shape, item.dtype) for item in arrays],
        in_specs=[pl.BlockSpec(memory_space=pltpu.HBM)] * len(arrays),
        out_specs=[pl.BlockSpec(memory_space=pltpu.VMEM)] * len(arrays),
        scratch_shapes=[pltpu.SemaphoreType.DMA((len(arrays),))],
        compiler_params=pltpu.CompilerParams(vmem_limit_bytes=24 << 20),
        cost_estimate=pl.CostEstimate(flops=0, bytes_accessed=8 << 20, transcendentals=0),
        name="load",
    )(*[pltpu.with_memory_space_constraint(item, pltpu.HBM) for item in arrays])


def call(kernel, out_shape, *args, scratch=(), smem=0, out_space=()):
    vmem = pl.BlockSpec(memory_space=pltpu.VMEM)
    in_specs = [pl.BlockSpec(memory_space=pltpu.SMEM)] * smem + [vmem] * (len(args) - smem)
    return pl.pallas_call(
        kernel,
        out_shape=[jax.ShapeDtypeStruct(*item) for item in out_shape],
        in_specs=in_specs,
        out_specs=[pl.BlockSpec(memory_space=space) for space in out_space or [pltpu.VMEM] * len(out_shape)],
        scratch_shapes=list(scratch),
        compiler_params=pltpu.CompilerParams(vmem_limit_bytes=24 << 20),
    )(*args)


def along(axis, values):
    rows, cols = lax.axis_size("ty"), lax.axis_size("tx")
    count, others = (rows, cols) if axis == "ty" else (cols, rows)

    def device(place, other, core):
        row, col = (place, other) if axis == "ty" else (other, place)
        return (row * cols + col) * 2 + core

    pairs = []
    for other in range(others):
        free = {device(place, other, core) for place in (0, count - 1) for core in range(2)}
        for place in range(count - 1):
            cores = (place % 2, place % 2) if axis == "ty" else (1, 0)
            one, two = device(place, other, cores[0]), device(place + 1, other, cores[1])
            pairs += [(one, two), (two, one)]
            free -= {one, two}
        if other % 2 == 0 and other + 1 < others:
            step = device(0, 1, 0) - device(0, 0, 0)
            for one in sorted(free):
                pairs += [(one, one + step), (one + step, one)]
    return lax.ppermute(values, ("ty", "tx", "corner"), pairs)


def ordered(axis, counts, mine, other):
    index, core = lax.axis_index(axis), lax.axis_index("corner")
    count = counts[axis]
    from_before = (core != lax.rem(index, 2)) if axis == "ty" else core == 0
    before = jnp.where(from_before, mine, other)
    after = jnp.where(from_before, other, mine)
    zero = jnp.zeros_like(mine)
    return jnp.where(index > 0, before, zero), jnp.where(index < count - 1, after, zero)


def across(values):
    return lax.ppermute(values, "corner", [(0, 1), (1, 0)])


def step(level_init, target, kernels, corner_doses):
    tile = level_init.shape[0]
    margin = HALO
    freqs = KF
    count = kernels.shape[1]
    tables = make_tables(tile, margin, freqs)
    bf16, f32 = jnp.bfloat16, jnp.float32
    counts = {"ty": lax.axis_size("ty"), "tx": lax.axis_size("tx")}
    edge = pl.pallas_call(
        edge_kernel,
        out_shape=jax.ShapeDtypeStruct((margin, tile), bf16),
        in_specs=[pl.BlockSpec(memory_space=pltpu.HBM)],
        out_specs=pl.BlockSpec(memory_space=pltpu.VMEM),
        scratch_shapes=[
            pltpu.VMEM((EDGE_PARTS, margin // EDGE_PARTS, tile), level_init.dtype),
            pltpu.SemaphoreType.DMA((EDGE_PARTS,)),
        ],
        compiler_params=pltpu.CompilerParams(vmem_limit_bytes=24 << 20),
        name="edge",
    )(pltpu.with_memory_space_constraint(level_init, pltpu.HBM))
    rows_mine = along("ty", edge)
    rows_other = across(rows_mine)
    names = sorted(tables)
    level_init, target, kernels, *loaded = load(
        level_init, target, kernels[0], *(tables[name] for name in names)
    )
    tables = dict(zip(names, loaded))
    strips = tile // margin * RIM
    packed = tables["packed"].shape[0]
    own_lift, strip = call(
        own_lift_kernel,
        [((packed, tile), f32), ((strips, margin), bf16)],
        level_init, tables["packed"],
    )
    (send,) = call(
        functools.partial(lift_kernel, counts),
        [((packed + strips + RIM, margin), bf16)],
        own_lift, strip, rows_mine, rows_other, tables["packed"],
    )
    cols_mine = along("tx", send)
    cols_other = across(cols_mine)
    (mixed,) = call(
        functools.partial(own_spec_kernel, counts),
        [((2 * freqs, 2 * freqs), f32)],
        own_lift, rows_mine, rows_other, tables["packed"], tables["expand"], tables["fwd_t"],
    )
    resist, grad = call(
        functools.partial(corner_kernel, counts),
        [((tile, tile), f32), ((2 * freqs, freqs), f32)],
        corner_doses, mixed, cols_mine, cols_other, kernels, target,
        tables["expand"], tables["fwd_t"], tables["inv"], tables["inv_t"],
        smem=1,
        scratch=[
            pltpu.VMEM((2 * freqs, count * freqs), bf16),
            pltpu.VMEM((tile, 2 * count * freqs), bf16),
            pltpu.VMEM((count, tile, 2 * tile), f32),
            pltpu.VMEM((2 * tile, count * freqs), bf16),
            pltpu.VMEM((tile, tile), f32),
            pltpu.SemaphoreType.DMA((BLOCKS,)),
        ],
        out_space=(pltpu.HBM, pltpu.VMEM),
    )
    grad = (grad + across(grad)).astype(bf16)
    grad_mine = along("tx", grad)
    grad_other = across(grad_mine)
    (own_grad,) = call(
        own_grad_kernel,
        [((2 * freqs, tile + margin), f32)],
        grad, tables["fwd"], tables["rim_cols"],
    )
    grad_lift, piece = call(
        functools.partial(lift_grad_kernel, counts),
        [((2 * freqs, tile + margin), bf16), ((margin + PAD, tile + margin), bf16)],
        own_grad, grad_mine, grad_other, tables["fwd"], tables["rim_cols"], tables["send_rows"],
    )
    piece_mine = along("ty", piece)
    piece_other = across(piece_mine)
    framed = (tile + RIM, tile + margin)
    levels = [pltpu.VMEM((framed[0] + 2 * PAD, margin), f32)] * (framed[1] // margin)
    frame = call(
        functools.partial(frame_kernel, counts),
        [(framed, f32)] * 4,
        grad_lift, tables["own_rows"], level_init, rows_mine, rows_other, cols_mine, cols_other,
        scratch=levels,
    )
    (level,) = call(
        functools.partial(advance_kernel, counts),
        [((tile, tile), f32)],
        frame[0], piece_mine, piece_other, *frame[1:],
        out_space=(pltpu.HBM,),
        scratch=[
            pltpu.VMEM(framed, f32),
            pltpu.VMEM((tile, tile), f32),
            pltpu.SemaphoreType.DMA((CHUNKS,)),
        ]
        + levels * 2,
    )
    return (resist[None], level)


def solution(mesh):
    in_specs = (P("ty", "tx"), P("ty", "tx"), P("corner", None, None, None, None), P("corner"))
    out_specs = (P("corner", "ty", "tx"), P("ty", "tx"))
    return jax.shard_map(step, mesh=mesh, in_specs=in_specs, out_specs=out_specs, check_vma=False)
```

```python
import functools
import math

import jax
import jax.numpy as jnp
import numpy as np
from jax import lax
from jax.experimental import pallas as pl
from jax.experimental.pallas import tpu as pltpu
from jax.sharding import PartitionSpec as P

HALO = 128
KF = 128
LS_STEPS = 3

STEEPNESS = 4.0
THRESHOLD = 1.0
SPEED_GAIN = 4.0
SMOOTHING = 0.24
GRAD_FLOOR = 0.25

RIM = 16
PAD = 8
CHUNKS = 4
BLOCKS = 1
EDGE_PARTS = 4


def make_tables(tile, margin, freqs):
    window = tile + 2 * margin
    shifts = np.arange(freqs) - freqs // 2
    places = np.arange(window)
    angles = 2.0 * math.pi / window * (shifts[:, None] * places[None, :] % window)
    scaled = 1.0 / math.sqrt(window)
    cos = np.cos(angles) * scaled
    sin = np.sin(angles) * scaled
    stacked = np.concatenate([cos, -sin], axis=0)
    inv_cos = cos[:, margin : margin + tile].T
    inv_sin = sin[:, margin : margin + tile].T
    inverse = np.block([[inv_cos, -inv_sin], [inv_sin, inv_cos]])

    def rim(width, offset):
        out = np.zeros((2 * freqs, width))
        for step in range(LS_STEPS):
            for place, at in ((tile + step, step), (step - LS_STEPS, width - LS_STEPS + step)):
                if 0 <= place + offset < window:
                    out[:, at] = stacked[:, place + offset]
        return out

    offsets = (margin + tile, margin, margin - tile)
    rim_cols = np.stack([rim(margin, offset) for offset in offsets])
    rim_rows = [rim(RIM, offset).T for offset in offsets]
    own_rows = stacked[:, margin : margin + tile].T
    own_rows = np.concatenate([rim_rows[1][PAD:], own_rows, rim_rows[1][:PAD]])
    send_rows = np.stack(
        [
            np.concatenate([stacked[:, :margin].T, rim_rows[2][:PAD]]),
            np.concatenate([rim_rows[0][PAD:], stacked[:, tile + margin :].T]),
        ]
    )
    half = freqs // 2
    packed = np.concatenate([stacked[:half], stacked[freqs : freqs + half], np.zeros((RIM, window))])
    packed[2 * half] = stacked[half]
    expand = np.zeros((2 * freqs, 2 * half + RIM))
    for row in range(freqs):
        mirror = row if row <= half else freqs - row
        expand[row, mirror if row != half else 2 * half] = 1.0
        if row != half:
            expand[freqs + row, half + mirror] = 1.0 if row < half else -1.0
    middle = slice(margin, margin + tile)
    by_place = np.concatenate([stacked[:, middle], stacked[:, :margin], stacked[:, tile + margin :]], 1).T
    as_const = lambda values: np.asarray(values, np.float32).astype(jnp.bfloat16)
    return {
        "fwd": as_const(stacked),
        "fwd_t": as_const(by_place),
        "packed": as_const(packed),
        "expand": as_const(expand),
        "inv": as_const(inverse),
        "inv_t": as_const(inverse.T),
        "rim_cols": as_const(rim_cols),
        "own_rows": as_const(own_rows),
        "send_rows": as_const(send_rows),
    }


def dot(left, right):
    return jnp.dot(left, right, preferred_element_type=jnp.float32)


def dot_general(left, right, left_dim, right_dim):
    return lax.dot_general(
        left, right, (((left_dim,), (right_dim,)), ((), ())), preferred_element_type=jnp.float32
    )


def by_core(core, first, second):
    return jnp.where(core == 0, first, second)


def edge_kernel(level_ref, edge_ref, buffer_ref, sems):
    margin = edge_ref.shape[0]
    part = margin // EDGE_PARTS
    place = 1 - lax.rem(lax.axis_index("corner") + lax.axis_index("ty"), 2)
    copies = []
    for at in range(EDGE_PARTS):
        rows = pl.ds(pl.multiple_of(place * margin + at * part, part), part)
        copies.append(
            pltpu.make_async_copy(level_ref.at[rows, :], buffer_ref.at[at], sems.at[at])
        )
        copies[-1].start()
    for at, copy in enumerate(copies):
        copy.wait()
        values = buffer_ref[at].astype(jnp.float32) * 0.125
        edge_ref[at * part : (at + 1) * part] = values.astype(jnp.bfloat16)


def squash(values):
    return jnp.tanh(0.25 * values).astype(jnp.bfloat16)


def rim_picker(margin):
    at = lax.broadcasted_iota(jnp.int32, (RIM, margin), 0)
    lane = lax.broadcasted_iota(jnp.int32, (RIM, margin), 1)
    first = by_core(lax.axis_index("corner"), 0, margin - LS_STEPS)
    return ((lane == first + at) & (at < LS_STEPS)).astype(jnp.bfloat16)


def own_lift_kernel(level_ref, packed_ref, lift_ref, strip_ref):
    core = lax.axis_index("corner")
    tile = level_ref.shape[0]
    margin = strip_ref.shape[1]
    level = level_ref[...].astype(jnp.float32) * 0.125
    lift_ref[...] = dot(packed_ref[:, margin : margin + tile], squash(level))
    strip = by_core(core, level[:, :margin], level[:, tile - margin :]).astype(jnp.bfloat16)
    pick = rim_picker(margin)
    for block in range(tile // margin):
        rows = strip[block * margin : (block + 1) * margin]
        picked = dot_general(pick, rows, 1, 1).astype(jnp.bfloat16)
        strip_ref[block * RIM : (block + 1) * RIM] = picked


def lift_kernel(counts, lift_ref, strip_ref, mine_ref, other_ref, packed_ref, send_ref):
    core = lax.axis_index("corner")
    margin, tile = mine_ref.shape
    rows = lift_ref.shape[0]
    lanes = pl.ds(pl.multiple_of(core * (tile - margin), margin), margin)
    above, below = ordered("ty", counts, mine_ref[:, lanes], other_ref[:, lanes])
    above = above.astype(jnp.float32)
    below = below.astype(jnp.float32)
    send_ref[:rows, :] = (
        lift_ref[:, lanes]
        + dot(packed_ref[:, :margin], squash(above))
        + dot(packed_ref[:, margin + tile :], squash(below))
    ).astype(jnp.bfloat16)
    strips = strip_ref.shape[0]
    send_ref[rows : rows + strips, :] = strip_ref[...]
    rim = jnp.where(
        lax.broadcasted_iota(jnp.int32, (RIM, margin), 0) < PAD, below[:RIM], above[margin - RIM :]
    )
    rim = jnp.concatenate([rim, jnp.zeros((margin - RIM, margin), jnp.float32)], axis=0)
    picked = dot_general(rim_picker(margin), rim.astype(jnp.bfloat16), 1, 1)
    send_ref[rows + strips :, :] = picked.astype(jnp.bfloat16)


def own_spec_kernel(
    counts, lift_ref, mine_ref, other_ref, packed_ref, expand_ref, fwd_t_ref, mixed_ref
):
    margin, tile = mine_ref.shape
    above, below = ordered("ty", counts, mine_ref[...], other_ref[...])
    lift = (
        lift_ref[...]
        + dot(packed_ref[:, :margin], squash(above.astype(jnp.float32)))
        + dot(packed_ref[:, margin + tile :], squash(below.astype(jnp.float32)))
    ).astype(jnp.bfloat16)
    lift = dot(expand_ref[...], lift).astype(jnp.bfloat16)
    mixed_ref[...] = dot(lift, fwd_t_ref[:tile])


def corner_kernel(
    counts,
    dose_ref,
    mixed_ref,
    mine_ref,
    other_ref,
    kernels_ref,
    target_ref,
    expand_ref,
    fwd_t_ref,
    inv_ref,
    inv_t_ref,
    resist_ref,
    grad_ref,
    blur_ref,
    proj_ref,
    field_ref,
    back_ref,
    done_ref,
    sems,
):
    tile = target_ref.shape[0]
    freqs = expand_ref.shape[0] // 2
    rows = expand_ref.shape[1]
    count = kernels_ref.shape[0]
    sides = ordered("tx", counts, mine_ref[:rows, :], other_ref[:rows, :])
    sides = dot(expand_ref[...], jnp.concatenate(sides, axis=1)).astype(jnp.bfloat16)
    mixed = mixed_ref[...] + dot(sides, fwd_t_ref[tile:])
    spec_re = mixed[:freqs, :freqs] - mixed[freqs:, freqs:]
    spec_im = mixed[:freqs, freqs:] + mixed[freqs:, :freqs]
    lanes = [slice(g * freqs, (g + 1) * freqs) for g in range(count)]
    groups = [range(g, min(g + 2, count)) for g in range(0, count, 2)]
    dose = dose_ref[0]
    size = tile // BLOCKS
    copies = []

    def project(group):
        for g in group:
            kernel_re = kernels_ref[g, 0]
            kernel_im = kernels_ref[g, 1]
            blur_re = (kernel_re * spec_re - kernel_im * spec_im).astype(jnp.bfloat16)
            blur_im = (kernel_re * spec_im + kernel_im * spec_re).astype(jnp.bfloat16)
            blur_ref[:freqs, lanes[g]] = blur_re
            blur_ref[freqs:, lanes[g]] = blur_im
        cols = slice(group[0] * freqs, (group[-1] + 1) * freqs)
        proj = dot(inv_ref[...], blur_ref[:, cols]).astype(jnp.bfloat16)
        for at, g in enumerate(group):
            for part in range(2):
                lane = (2 * g + part) * freqs
                proj_ref[:, lane : lane + freqs] = proj[part * tile : (part + 1) * tile, lanes[at]]

    def forward(block, g):
        at = slice(block * size, (block + 1) * size)
        pair = proj_ref[at, 2 * g * freqs : 2 * (g + 1) * freqs]
        field_ref[g, at] = dot(pair, inv_t_ref[...])

    def sensitivity(block):
        at = slice(block * size, (block + 1) * size)
        power = None
        for g in range(count):
            field = field_ref[g, at]
            term = field[:, :tile] * field[:, :tile] + field[:, tile:] * field[:, tile:]
            power = term if power is None else power + term
        resist = jax.nn.sigmoid(STEEPNESS * (dose * power - THRESHOLD))
        done_ref[at] = resist
        copies.append(
            pltpu.make_async_copy(done_ref.at[at, :], resist_ref.at[at, :], sems.at[block])
        )
        copies[-1].start()
        goal = target_ref[at].astype(jnp.float32)
        return (4.0 * STEEPNESS * dose) * (resist - goal) * (resist * (1.0 - resist))

    def backward(block, g, twice):
        at = slice(block * size, (block + 1) * size)
        adj_re = (twice * field_ref[g, at, :tile]).astype(jnp.bfloat16)
        adj_im = (twice * field_ref[g, at, tile:]).astype(jnp.bfloat16)
        adj = jnp.concatenate([adj_re, adj_im], axis=1)
        back = dot(adj, inv_ref[...]).astype(jnp.bfloat16)
        back_ref[block * size : (block + 1) * size, lanes[g]] = back[:, :freqs]
        back_ref[tile + block * size : tile + (block + 1) * size, lanes[g]] = back[:, freqs:]

    for group in groups:
        project(group)
    for g in range(count):
        forward(0, g)
    for block in range(BLOCKS):
        twice = sensitivity(block)
        for g in range(count):
            if block + 1 < BLOCKS:
                forward(block + 1, g)
        for g in range(count):
            backward(block, g, twice)
    grad_re = None
    for group in groups:
        cols = slice(group[0] * freqs, (group[-1] + 1) * freqs)
        blurred = dot(inv_t_ref[...], back_ref[:, cols])
        for at, g in enumerate(group):
            kernel_re = kernels_ref[g, 0]
            kernel_im = kernels_ref[g, 1]
            blur_re = blurred[:freqs, lanes[at]]
            blur_im = blurred[freqs:, lanes[at]]
            term_re = kernel_re * blur_re + kernel_im * blur_im
            term_im = kernel_re * blur_im - kernel_im * blur_re
            grad_re = term_re if grad_re is None else grad_re + term_re
            grad_im = term_im if g == 0 else grad_im + term_im
    grad_ref[:freqs, :] = grad_re
    grad_ref[freqs:, :] = grad_im
    for copy in copies:
        copy.wait()


def both_parts(values):
    freqs = values.shape[0] // 2
    low_re = values[:freqs]
    low_im = values[freqs:]
    upper = jnp.concatenate([low_re, low_im], axis=1)
    lower = jnp.concatenate([low_im, -low_re], axis=1)
    return jnp.concatenate([upper, lower], axis=0)


def own_grad_kernel(grad_ref, fwd_ref, rim_ref, lift_ref):
    margin = rim_ref.shape[2]
    tile = fwd_ref.shape[1] - 2 * margin
    here = both_parts(grad_ref[...])
    lift_ref[:, :tile] = dot(here, fwd_ref[:, margin : margin + tile])
    lift_ref[:, tile:] = dot(here, rim_ref[1])


def lift_grad_kernel(
    counts, own_ref, mine_ref, other_ref, fwd_ref, rim_ref, send_rows_ref, lift_ref, send_ref
):
    to_after = 1 - lax.rem(lax.axis_index("corner") + lax.axis_index("ty"), 2)
    margin = rim_ref.shape[2]
    tile = fwd_ref.shape[1] - 2 * margin
    before, after = ordered("tx", counts, mine_ref[...], other_ref[...])
    before = both_parts(before)
    after = both_parts(after)
    first = own_ref[:, :margin] + dot(before, fwd_ref[:, tile + margin :])
    last = own_ref[:, tile - margin : tile] + dot(after, fwd_ref[:, :margin])
    rim = own_ref[:, tile:] + dot(before, rim_ref[0]) + dot(after, rim_ref[2])
    lift_ref[:, :margin] = first.astype(jnp.bfloat16)
    lift_ref[:, tile - margin : tile] = last.astype(jnp.bfloat16)
    lift_ref[:, tile:] = rim.astype(jnp.bfloat16)
    send_ref[...] = dot(send_rows_ref[to_after], lift_ref[...]).astype(jnp.bfloat16)


def stencil(source, at, wanted, margin):
    blocks = len(source)
    lane = lax.broadcasted_iota(jnp.int32, (PAD, margin), 1)
    here = [ref[PAD + at : 2 * PAD + at] for ref in source]
    back = [pltpu.roll(part, 1, 1) for part in here]
    ahead = [pltpu.roll(part, margin - 1, 1) for part in here]
    for block in range(wanted):
        up = source[block][PAD + at - 1 : 2 * PAD + at - 1]
        down = source[block][PAD + at + 1 : 2 * PAD + at + 1]
        left = jnp.where(lane == 0, back[block - 1], back[block])
        right = jnp.where(lane == margin - 1, ahead[(block + 1) % blocks], ahead[block])
        slope_y = down - up
        slope_x = right - left
        square = GRAD_FLOOR + slope_y * slope_y + slope_x * slope_x
        base = (1.0 - 4.0 * SMOOTHING) * here[block] + SMOOTHING * ((up + down) + (left + right))
        yield base, square * lax.rsqrt(square)


def frame_kernel(
    counts,
    lift_ref, own_rows_ref, level_ref, mine_ref, other_ref, cols_mine_ref, cols_other_ref,
    grad_ref, slope_ref, base_ref, root_ref, *level_refs,
):
    tile = level_ref.shape[0]
    margin = mine_ref.shape[0]
    grad_ref[...] = dot(own_rows_ref[...], lift_ref[...])
    rows = cols_mine_ref.shape[0] - (tile // margin + 1) * RIM
    above, below = ordered("ty", counts, mine_ref[...], other_ref[...])
    blocks = len(level_refs)
    extent = slope_ref.shape[0]
    level = level_ref[...].astype(jnp.float32) * 0.0625
    above = 0.5 * above.astype(jnp.float32)[margin - PAD :]
    below = 0.5 * below.astype(jnp.float32)[:PAD]
    zero = jnp.zeros((PAD, margin), jnp.float32)
    for block, ref in enumerate(level_refs):
        ref[:PAD] = zero
        ref[PAD + extent :] = zero
        if block < blocks - 1:
            lanes = slice(block * margin, (block + 1) * margin)
            ref[PAD : 2 * PAD] = above[:, lanes]
            ref[2 * PAD : 2 * PAD + tile] = level[:, lanes]
            ref[2 * PAD + tile : PAD + extent] = below[:, lanes]
    at = lax.broadcasted_iota(jnp.int32, (RIM, margin), 0)
    lane = lax.broadcasted_iota(jnp.int32, (RIM, margin), 1)
    place_left = ((lane == margin - LS_STEPS + at) & (at < LS_STEPS)).astype(jnp.bfloat16)
    place_right = ((lane == at) & (at < LS_STEPS)).astype(jnp.bfloat16)
    side = level_refs[-1]
    for block in range(tile // margin + 1):
        part = slice(rows + block * RIM, rows + (block + 1) * RIM)
        left, right = ordered("tx", counts, cols_mine_ref[part, :], cols_other_ref[part, :])
        placed = dot_general(left, place_left, 0, 0) + dot_general(right, place_right, 0, 0)
        placed = 0.5 * placed
        if block < tile // margin:
            start = 2 * PAD + block * margin
            side[start : start + margin] = placed
        else:
            side[2 * PAD + tile : PAD + extent] = placed[:PAD]
            side[PAD : 2 * PAD] = placed[PAD:RIM]
    for at in range(0, extent, PAD):
        for block, (base, root) in enumerate(stencil(level_refs, at, blocks, margin)):
            lanes = slice(block * margin, (block + 1) * margin)
            trans = jnp.tanh(0.5 * level_refs[block][PAD + at : 2 * PAD + at])
            base_ref[at : at + PAD, lanes] = base
            root_ref[at : at + PAD, lanes] = root
            slope_ref[at : at + PAD, lanes] = (SPEED_GAIN * 0.5 * 0.25) * (1.0 - trans * trans)


def half_of_piece():
    return lax.rem(lax.axis_index("corner") + lax.axis_index("ty") + 1, 2)


def valid_piece(counts, half, piece):
    at_ty = lax.axis_index("ty")
    inside = jnp.where(half == 0, at_ty, counts["ty"] - 1 - at_ty) > 0
    return jnp.where(inside, piece, jnp.zeros_like(piece)).astype(jnp.float32)


def advance_rows(counts, start, size, speed_ref, base_ref, root_ref, level_refs, store):
    rows, cols = base_ref.shape
    blocks = len(level_refs) // 2
    margin = cols // blocks
    lane = lax.broadcasted_iota(jnp.int32, (PAD, margin), 1)
    at_ty, at_tx = lax.axis_index("ty"), lax.axis_index("tx")
    every = lane >= 0
    above = every & (at_ty + start > 0)
    below = every & (counts["ty"] - 1 - at_ty + (rows - size - start) > 0)
    beside = ((lane >= margin // 2) & (at_tx > 0)) | (
        (lane < margin // 2) & (at_tx < counts["tx"] - 1)
    )
    for ref in level_refs:
        ref[:PAD] = jnp.zeros((PAD, margin), jnp.float32)
        ref[PAD + size : 2 * PAD + size] = jnp.zeros((PAD, margin), jnp.float32)
    source, target = level_refs[:blocks], level_refs[blocks:]
    for step in range(LS_STEPS):
        final = step == LS_STEPS - 1
        for at in range(PAD if final else 0, size - PAD if final else size, PAD):
            here = pl.ds(pl.multiple_of(start + at, PAD), PAD)
            lanes = [slice(block * margin, (block + 1) * margin) for block in range(blocks)]
            if step == 0:
                parts = [(base_ref[here, cut], root_ref[here, cut]) for cut in lanes]
            else:
                parts = stencil(source, at, blocks - 1 if final else blocks, margin)
            for block, (base, root) in enumerate(parts):
                level = base - speed_ref[at : at + PAD, lanes[block]] * root
                if final:
                    store(at, lanes[block], 2.0 * level)
                    continue
                if at == 0:
                    level = jnp.where(above, level, 0.0)
                if at == size - PAD:
                    level = jnp.where(below, level, 0.0)
                if block == blocks - 1:
                    level = jnp.where(beside, level, 0.0)
                target[block][PAD + at : 2 * PAD + at] = level
        source, target = target, source


def advance_mine_kernel(
    counts, grad_ref, mine_ref, slope_ref, base_ref, root_ref, speed_ref, done_ref, *level_refs
):
    half = half_of_piece()
    size = mine_ref.shape[0]
    start = half * (grad_ref.shape[0] - size)
    here = pl.ds(pl.multiple_of(start, PAD), size)
    piece = valid_piece(counts, half, mine_ref[...])
    speed_ref[...] = (grad_ref[here, :] + piece) * slope_ref[here, :]

    def store(at, lanes, level):
        done_ref[at - PAD : at, lanes] = level

    advance_rows(counts, start, size, speed_ref, base_ref, root_ref, level_refs, store)


def advance_rest_kernel(
    counts, grad_ref, other_ref, slope_ref, base_ref, root_ref, mine_speed_ref, mine_ref, out_ref,
    speed_ref, done_ref, sems, *level_refs,
):
    half = half_of_piece()
    size = other_ref.shape[0]
    rows = mine_ref.shape[0]
    rest = out_ref.shape[0] - rows
    place = pl.ds(pl.multiple_of(half * rest, PAD), rows)
    copies = [pltpu.make_async_copy(mine_ref, out_ref.at[place, :], sems.at[0])]
    copies[0].start()
    here = pl.ds(pl.multiple_of((1 - half) * (grad_ref.shape[0] - size), PAD), size)
    piece = valid_piece(counts, 1 - half, other_ref[...])
    target = pl.ds(pl.multiple_of((1 - half) * 2 * PAD, PAD), size)
    speed_ref[target, :] = (grad_ref[here, :] + piece) * slope_ref[here, :]
    source = pl.ds(pl.multiple_of((1 - half) * (size - 2 * PAD), PAD), 2 * PAD)
    target = pl.ds(pl.multiple_of(half * size, PAD), 2 * PAD)
    speed_ref[target, :] = mine_speed_ref[source, :]
    first = (1 - half) * rows

    def store(at, lanes, level):
        done_ref[at - PAD : at, lanes] = level
        chunk = rest // CHUNKS // PAD * PAD
        if lanes.start == 0 or (at % chunk and at != rest):
            return
        begin = (at - 1) // chunk * chunk
        target = pl.ds(pl.multiple_of(first + begin, PAD), at - begin)
        copy = pltpu.make_async_copy(
            done_ref.at[begin:at, :], out_ref.at[target, :], sems.at[len(copies)]
        )
        copy.start()
        copies.append(copy)

    start = (1 - half) * (grad_ref.shape[0] - size - 2 * PAD)
    advance_rows(counts, start, size + 2 * PAD, speed_ref, base_ref, root_ref, level_refs, store)
    for copy in copies:
        copy.wait()


def load_kernel(*refs):
    count = len(refs) // 2
    sems = refs[-1]
    copies = [
        pltpu.make_async_copy(refs[i], refs[count + i], sems.at[i]) for i in range(count)
    ]
    for copy in copies:
        copy.start()
    for copy in copies:
        copy.wait()


def load(*arrays):
    return pl.pallas_call(
        load_kernel,
        out_shape=[jax.ShapeDtypeStruct(item.shape, item.dtype) for item in arrays],
        in_specs=[pl.BlockSpec(memory_space=pltpu.HBM)] * len(arrays),
        out_specs=[pl.BlockSpec(memory_space=pltpu.VMEM)] * len(arrays),
        scratch_shapes=[pltpu.SemaphoreType.DMA((len(arrays),))],
        compiler_params=pltpu.CompilerParams(vmem_limit_bytes=24 << 20),
        cost_estimate=pl.CostEstimate(flops=0, bytes_accessed=8 << 20, transcendentals=0),
        name="load",
    )(*[pltpu.with_memory_space_constraint(item, pltpu.HBM) for item in arrays])


def call(kernel, out_shape, *args, scratch=(), smem=0, out_space=()):
    vmem = pl.BlockSpec(memory_space=pltpu.VMEM)
    in_specs = [pl.BlockSpec(memory_space=pltpu.SMEM)] * smem + [vmem] * (len(args) - smem)
    return pl.pallas_call(
        kernel,
        out_shape=[jax.ShapeDtypeStruct(*item) for item in out_shape],
        in_specs=in_specs,
        out_specs=[pl.BlockSpec(memory_space=space) for space in out_space or [pltpu.VMEM] * len(out_shape)],
        scratch_shapes=list(scratch),
        compiler_params=pltpu.CompilerParams(vmem_limit_bytes=24 << 20),
    )(*args)


def along(axis, values):
    rows, cols = lax.axis_size("ty"), lax.axis_size("tx")
    count, others = (rows, cols) if axis == "ty" else (cols, rows)

    def device(place, other, core):
        row, col = (place, other) if axis == "ty" else (other, place)
        return (row * cols + col) * 2 + core

    pairs = []
    for other in range(others):
        free = {device(place, other, core) for place in (0, count - 1) for core in range(2)}
        for place in range(count - 1):
            cores = (place % 2, place % 2) if axis == "ty" else (1, 0)
            one, two = device(place, other, cores[0]), device(place + 1, other, cores[1])
            pairs += [(one, two), (two, one)]
            free -= {one, two}
        if other % 2 == 0 and other + 1 < others:
            step = device(0, 1, 0) - device(0, 0, 0)
            for one in sorted(free):
                pairs += [(one, one + step), (one + step, one)]
    return lax.ppermute(values, ("ty", "tx", "corner"), pairs)


def ordered(axis, counts, mine, other):
    index, core = lax.axis_index(axis), lax.axis_index("corner")
    count = counts[axis]
    from_before = (core != lax.rem(index, 2)) if axis == "ty" else core == 0
    before = jnp.where(from_before, mine, other)
    after = jnp.where(from_before, other, mine)
    zero = jnp.zeros_like(mine)
    return jnp.where(index > 0, before, zero), jnp.where(index < count - 1, after, zero)


def across(values):
    return lax.ppermute(values, "corner", [(0, 1), (1, 0)])


def step(level_init, target, kernels, corner_doses):
    tile = level_init.shape[0]
    margin = HALO
    freqs = KF
    count = kernels.shape[1]
    tables = make_tables(tile, margin, freqs)
    bf16, f32 = jnp.bfloat16, jnp.float32
    counts = {"ty": lax.axis_size("ty"), "tx": lax.axis_size("tx")}
    edge = pl.pallas_call(
        edge_kernel,
        out_shape=jax.ShapeDtypeStruct((margin, tile), bf16),
        in_specs=[pl.BlockSpec(memory_space=pltpu.HBM)],
        out_specs=pl.BlockSpec(memory_space=pltpu.VMEM),
        scratch_shapes=[
            pltpu.VMEM((EDGE_PARTS, margin // EDGE_PARTS, tile), level_init.dtype),
            pltpu.SemaphoreType.DMA((EDGE_PARTS,)),
        ],
        compiler_params=pltpu.CompilerParams(vmem_limit_bytes=24 << 20),
        name="edge",
    )(pltpu.with_memory_space_constraint(level_init, pltpu.HBM))
    rows_mine = along("ty", edge)
    rows_other = across(rows_mine)
    names = sorted(tables)
    level_init, target, kernels, *loaded = load(
        level_init, target, kernels[0], *(tables[name] for name in names)
    )
    tables = dict(zip(names, loaded))
    strips = tile // margin * RIM
    packed = tables["packed"].shape[0]
    own_lift, strip = call(
        own_lift_kernel,
        [((packed, tile), f32), ((strips, margin), bf16)],
        level_init, tables["packed"],
    )
    (send,) = call(
        functools.partial(lift_kernel, counts),
        [((packed + strips + RIM, margin), bf16)],
        own_lift, strip, rows_mine, rows_other, tables["packed"],
    )
    cols_mine = along("tx", send)
    cols_other = across(cols_mine)
    (mixed,) = call(
        functools.partial(own_spec_kernel, counts),
        [((2 * freqs, 2 * freqs), f32)],
        own_lift, rows_mine, rows_other, tables["packed"], tables["expand"], tables["fwd_t"],
    )
    resist, grad = call(
        functools.partial(corner_kernel, counts),
        [((tile, tile), f32), ((2 * freqs, freqs), f32)],
        corner_doses, mixed, cols_mine, cols_other, kernels, target,
        tables["expand"], tables["fwd_t"], tables["inv"], tables["inv_t"],
        smem=1,
        scratch=[
            pltpu.VMEM((2 * freqs, count * freqs), bf16),
            pltpu.VMEM((tile, 2 * count * freqs), bf16),
            pltpu.VMEM((count, tile, 2 * tile), f32),
            pltpu.VMEM((2 * tile, count * freqs), bf16),
            pltpu.VMEM((tile, tile), f32),
            pltpu.SemaphoreType.DMA((BLOCKS,)),
        ],
        out_space=(pltpu.HBM, pltpu.VMEM),
    )
    grad = (grad + across(grad)).astype(bf16)
    grad_mine = along("tx", grad)
    grad_other = across(grad_mine)
    (own_grad,) = call(
        own_grad_kernel,
        [((2 * freqs, tile + margin), f32)],
        grad, tables["fwd"], tables["rim_cols"],
    )
    grad_lift, piece = call(
        functools.partial(lift_grad_kernel, counts),
        [((2 * freqs, tile + margin), bf16), ((margin + PAD, tile + margin), bf16)],
        own_grad, grad_mine, grad_other, tables["fwd"], tables["rim_cols"], tables["send_rows"],
    )
    piece_mine = along("ty", piece)
    piece_other = across(piece_mine)
    framed = (tile + RIM, tile + margin)
    levels = [pltpu.VMEM((framed[0] + 2 * PAD, margin), f32)] * (framed[1] // margin)
    frame = call(
        functools.partial(frame_kernel, counts),
        [(framed, f32)] * 4,
        grad_lift, tables["own_rows"], level_init, rows_mine, rows_other, cols_mine, cols_other,
        scratch=levels,
    )
    own_piece, frame = frame[0], frame[1:]
    mine_rows = margin + PAD
    done_rows = mine_rows - 2 * PAD
    rest_rows = mine_rows + 2 * PAD

    def levels_of(size):
        return [pltpu.VMEM((size + 2 * PAD, margin), f32)] * (2 * framed[1] // margin)

    mine_speed, mine_done = call(
        functools.partial(advance_mine_kernel, counts),
        [((mine_rows, framed[1]), f32), ((done_rows, tile), f32)],
        own_piece, piece_mine, *frame,
        scratch=levels_of(mine_rows),
    )
    (level,) = call(
        functools.partial(advance_rest_kernel, counts),
        [((tile, tile), f32)],
        own_piece, piece_other, *frame, mine_speed, mine_done,
        out_space=(pltpu.HBM,),
        scratch=[
            pltpu.VMEM((rest_rows, framed[1]), f32),
            pltpu.VMEM((tile - done_rows, tile), f32),
            pltpu.SemaphoreType.DMA((CHUNKS + 2,)),
        ]
        + levels_of(rest_rows),
    )
    return (resist[None], level)


def solution(mesh):
    in_specs = (P("ty", "tx"), P("ty", "tx"), P("corner", None, None, None, None), P("corner"))
    out_specs = (P("corner", "ty", "tx"), P("ty", "tx"))
    return jax.shard_map(step, mesh=mesh, in_specs=in_specs, out_specs=out_specs, check_vma=False)
```
